256 devices in a mesh: section: 4 (over y_lo, core), expert: 64 (over z, x, y_hi).
Axes of the slice: x: 4, y: 4 (y_hi: 2, y_lo: 2; y = y_hi * 2 + y_lo), z: 8, core: 2. Of those that a mesh axis runs over, the one named last changes fastest.
Arguments:
- tokens: bfloat16 [4, 8192, 2048], P('section', 'expert'), may hold values from -6 to 6
- cotangent: bfloat16 [4, 8192, 2048], P('section', 'expert'), may hold values from -3 to 3
- routes: int32 [4, 8192, 8], P('section', 'expert'), may hold values from 0 to 63, all different within a row; in each aligned block of 128 rows (0 to 127, 128 to 255, ..., all dimensions but the last counted through in order) at most 18 rows name the same one
- route_weights: bfloat16 [4, 8192, 8], P('section', 'expert'), may hold values from 0.099609375 to 1
- weights: bfloat16 [3, 64, 2048, 384], P(None, 'expert'), may hold values from -0.125 to 0.125
Outputs:
- token_grads: bfloat16 [4, 8192, 2048], P('section', 'expert')
- gate_grads: bfloat16 [4, 8192, 8], P('section', 'expert')
- weight_grads: float32 [3, 64, 2048, 384], P(None, 'expert', 'section')
The draws below stay inside these ranges and needn't reach their ends.
Inputs may be any that keep to these rules, and one draw needn't show every extreme that they name: `routes`: the 8 experts of a token differ. Among the 128 tokens of one device no expert is named more than 18 times, a bound that some block reaches.
All inputs are finite; a program needn't handle non-finite values.
Results may differ from the reference program's by a relative error of at most 0.0085.
Values may be sent and summed in bfloat16 or wider, within the bound.
No kernel may reach another device: no remote copies, remote signals or barrier semaphores. Data moves between devices by JAX's collectives and lax.ppermute only.
A program may use at most 128 MiB of HBM per device.

```python
import math
import jax
import jax.numpy as jnp
import numpy as np
from jax import lax

D = 2048
FF = 384
TOP_K = 8
TOK_DEV = 128
EXPERTS = 64
CAP = 18
TOKENS = 8192
N_SECTION = 4
N_EXPERT = 64


def steps_of(stream_key, shape, split, least, high):
    gain = 1.0
    for dim, parts in split:
        heights = jax.random.uniform(jax.random.fold_in(jax.random.fold_in(stream_key, 6), dim), (parts,), jnp.float32, least / len(split), high / len(split))
        gain = gain * jnp.repeat(jnp.exp(heights), shape[dim] // parts).reshape((-1,) + (1,) * (len(shape) - 1 - dim))
    return gain


def assign_block(stream_key, own, number, rows, count, top, reach, lean):
    sequence = jax.random.permutation(stream_key, count)
    crowded, ordinary = load_shares(count, rows * top, reach, lean, True), load_shares(count, rows * top, reach, lean, False)
    places = jnp.arange(count)

    def named(lengths, offset_by):
        used = int((lengths > 0).sum())
        fixed = max(1, used // 4)
        moved = fixed + (places - fixed + offset_by * (used - fixed)) % max(1, count - fixed)
        return jnp.zeros((count,), jnp.int32).at[sequence[jnp.where(places < fixed, places, moved)]].set(jnp.asarray(lengths, jnp.int32))

    lengths = jnp.where(number % 4 == 0, named(crowded, number // 4), named(ordinary, number - number // 4 - 1))
    mixed = jax.random.permutation(jax.random.fold_in(own, 3), count)
    donor, sink = mixed[0:count // 2 * 2:2], mixed[1:count // 2 * 2:2]
    margin = jnp.minimum(lengths[donor] - 1, reach - lengths[sink]) // 2
    margin = jnp.where((donor == sequence[0]) | (sink == sequence[0]) | (lengths[sink] == 0), 0, jnp.maximum(margin, 0))
    moved = jax.random.randint(jax.random.fold_in(own, 4), (count // 2,), 0, 1 << 20) % (margin + 1)
    lengths = lengths.at[donor].add(-moved).at[sink].add(moved)
    labels = jnp.searchsorted(jnp.cumsum(lengths), jnp.arange(rows * top), side="right").astype(jnp.int32)
    grid = labels.reshape(top, rows).T
    grid = grid[jax.random.permutation(jax.random.fold_in(own, 1), rows)]
    offset_by = jax.random.randint(jax.random.fold_in(own, 2), (rows, 1), 0, top)
    return jnp.take_along_axis(grid, (jnp.arange(top)[None, :] + offset_by) % top, axis=1)


def load_shares(number_of, total, reach, lean, full):
    portions = [(1 << 20) // math.isqrt(standing ** lean) + 1 for standing in range(1, number_of + 1)]
    largest = reach if full else min(reach, max(-(-total // number_of), total * portions[0] // sum(portions)))
    least = 1 if total - largest >= number_of - 1 else 0
    given, rest = [largest] + [least] * (number_of - 1), total - largest - least * (number_of - 1)
    while rest > 0:
        candidates = [i for i in range(1, number_of) if given[i] < largest] or [i for i in range(1, number_of) if given[i] < reach]
        pool, remaining = sum([portions[i] for i in candidates]), rest
        for i in candidates:
            more = min(reach - given[i], max(1, remaining * portions[i] // pool), rest)
            given[i] = given[i] + more
            rest = rest - more
    return np.array(given)


def bell_draw(rng, dims, scale, most, cuts=(), kind=jnp.bfloat16):
    entries = jax.random.normal(rng, dims, jnp.float32) * scale
    if len(cuts) > 0:
        entries = steps_of(rng, dims, cuts, -0.22, 0.18) * entries
    return jnp.clip(entries, min=-most, max=most).astype(kind)


def setup_inputs(seed: int = 0) -> dict:
    arg_keys = jax.random.split(jax.random.key(seed), 6)
    tokens = bell_draw(arg_keys[0], (N_SECTION, TOKENS, D), 1.0, 6.0, ((0, 4), (1, 64)))
    cotangent = bell_draw(arg_keys[1], (N_SECTION, TOKENS, D), 0.5, 3.0, ((0, 4), (1, 64)))
    routes_keys = jax.random.split(jax.random.fold_in(arg_keys[2], 1), N_SECTION * TOKENS // TOK_DEV)
    routes_turns = jax.random.permutation(jax.random.fold_in(arg_keys[2], 3), N_SECTION * TOKENS // TOK_DEV)
    routes = jax.vmap(lambda own, number: assign_block(jax.random.fold_in(arg_keys[2], 2), own, number, TOK_DEV, EXPERTS, TOP_K, CAP, 1))(routes_keys, routes_turns).reshape((N_SECTION, TOKENS, TOP_K))
    route_weights = jnp.clip(jnp.exp(math.log(1.0) - 2.306499 * jax.random.uniform(arg_keys[3], (N_SECTION, TOKENS, TOP_K), jnp.float32) ** steps_of(arg_keys[3], (N_SECTION, TOKENS, TOP_K), ((0, 4), (1, 64)), -0.2, 0.2)), 0.099609375, 1.0).astype(jnp.bfloat16)
    weights = bell_draw(arg_keys[4], (3, EXPERTS, D, FF), D ** -0.5, 0.125, ((1, 64),))
    return {"tokens": tokens, "cotangent": cotangent, "routes": routes, "route_weights": route_weights, "weights": weights}


def slot_assign(route_block, experts, capacity):
    flat_ids = route_block.reshape(-1)
    pair_count = flat_ids.shape[0]
    one_hot = (flat_ids[:, None] == jnp.arange(experts, dtype=jnp.int32)[None, :]).astype(jnp.int32)
    before = jnp.cumsum(one_hot, axis=0) - one_hot
    slot_of = jnp.sum(before * one_hot, axis=1).astype(jnp.int32)
    slot_table = jnp.full((experts, capacity), pair_count, jnp.int32)
    slot_table = slot_table.at[flat_ids, slot_of].set(jnp.arange(pair_count, dtype=jnp.int32))
    return slot_of.reshape(route_block.shape), slot_table


def expert_step(in_rows, cot_rows, weight_rows, expert_w):
    gate_pre = jnp.dot(in_rows, expert_w[0], preferred_element_type=jnp.float32)
    up_pre = jnp.dot(in_rows, expert_w[1], preferred_element_type=jnp.float32)
    sigmoid_v = jax.nn.sigmoid(gate_pre)
    silu_v = gate_pre * sigmoid_v
    hidden = (silu_v * up_pre).astype(jnp.bfloat16)
    back_proj = jnp.dot(cot_rows, expert_w[2], preferred_element_type=jnp.float32)
    row_gate = jnp.sum(hidden.astype(jnp.float32) * back_proj, axis=1).astype(jnp.bfloat16)
    weight = weight_rows.astype(jnp.float32)[:, None]
    d_hidden = weight * back_proj
    d_gate_pre = (d_hidden * up_pre * sigmoid_v * (1.0 + gate_pre * (1.0 - sigmoid_v))).astype(jnp.bfloat16)
    d_up_pre = (d_hidden * silu_v).astype(jnp.bfloat16)
    scaled = (weight * cot_rows.astype(jnp.float32)).astype(jnp.bfloat16)
    contract_rows = (((0,), (0,)), ((), ()))
    weight_part = jnp.stack([
        lax.dot_general(in_rows, d_gate_pre, contract_rows, preferred_element_type=jnp.float32),
        lax.dot_general(in_rows, d_up_pre, contract_rows, preferred_element_type=jnp.float32),
        lax.dot_general(scaled, hidden, contract_rows, preferred_element_type=jnp.float32)])
    contract_ff = (((1,), (1,)), ((), ()))
    row_grads = (lax.dot_general(d_gate_pre, expert_w[0], contract_ff, preferred_element_type=jnp.float32)
                 + lax.dot_general(d_up_pre, expert_w[1], contract_ff, preferred_element_type=jnp.float32)).astype(jnp.bfloat16)
    return row_gate, row_grads, weight_part


def reference(tokens, cotangent, routes, route_weights, weights):
    blocks = N_EXPERT
    route_blocks = routes.reshape(N_SECTION, blocks, TOK_DEV, TOP_K)
    slots, tables = jax.vmap(jax.vmap(lambda route_block: slot_assign(route_block, EXPERTS, CAP)))(route_blocks)
    zero_row = jnp.zeros((N_SECTION, blocks, 1, D), tokens.dtype)
    tok_pad = jnp.concatenate([tokens.reshape(N_SECTION, blocks, TOK_DEV, D), zero_row], axis=2)
    cot_pad = jnp.concatenate([cotangent.reshape(N_SECTION, blocks, TOK_DEV, D), zero_row.astype(cotangent.dtype)], axis=2)
    gate_pad = jnp.concatenate([route_weights.reshape(N_SECTION, blocks, TOK_DEV * TOP_K),
                                jnp.zeros((N_SECTION, blocks, 1), route_weights.dtype)], axis=2)
    section_ix = jnp.arange(N_SECTION, dtype=jnp.int32)[:, None, None]
    block_ix = jnp.arange(blocks, dtype=jnp.int32)[None, :, None]

    def per_expert(expert):
        slot_table = tables[:, :, expert, :]
        token_ix = slot_table // TOP_K
        rows_all = tok_pad[section_ix, block_ix, token_ix]
        cots_all = cot_pad[section_ix, block_ix, token_ix]
        gate_vals = gate_pad[section_ix, block_ix, slot_table]
        expert_w = weights[:, expert]
        accum = jnp.zeros((3, D, FF), jnp.float32)
        gate_list = []
        row_list = []
        for section_no in range(N_SECTION):
            row_gate, row_grads, weight_part = expert_step(
                rows_all[section_no].reshape(-1, D), cots_all[section_no].reshape(-1, D),
                gate_vals[section_no].reshape(-1), expert_w)
            rounded = lax.optimization_barrier(weight_part.astype(jnp.bfloat16))
            accum = accum + rounded.astype(jnp.float32)
            gate_list.append(row_gate.reshape(blocks, CAP))
            row_list.append(row_grads.reshape(blocks, CAP, D))
        return jnp.stack(gate_list), jnp.stack(row_list), accum / N_SECTION

    gate_back, row_back, grads_all = lax.map(per_expert, jnp.arange(EXPERTS, dtype=jnp.int32))
    section_four = jnp.arange(N_SECTION, dtype=jnp.int32)[:, None, None]
    block_four = jnp.arange(blocks, dtype=jnp.int32)[None, :, None]
    accum = jnp.zeros((N_SECTION, blocks, TOK_DEV, D), jnp.float32)
    for position in range(TOP_K):
        accum = accum + row_back[route_blocks[..., position], section_four, block_four, slots[..., position]].astype(jnp.float32)
    token_grads = accum.astype(jnp.bfloat16).reshape(N_SECTION, TOKENS, D)
    section_five = jnp.arange(N_SECTION, dtype=jnp.int32)[:, None, None, None]
    block_five = jnp.arange(blocks, dtype=jnp.int32)[None, :, None, None]
    gate_grads = gate_back[route_blocks, section_five, block_five, slots].reshape(N_SECTION, TOKENS, TOP_K)
    weight_grads = jnp.transpose(grads_all, (1, 0, 2, 3))
    return token_grads, gate_grads, weight_grads
```

```python
import functools

import jax
import jax.numpy as jnp
from jax import lax
from jax.experimental import pallas as pl
from jax.experimental.pallas import tpu as pltpu
from jax.sharding import PartitionSpec as P

D = 2048
FF = 384
TOP_K = 8
TOK = 128
CAP = 18
PLANES = 8
PLANE = 8
META = 8
ROWS = TOK + META
HALF = 64
NEAR = (0, -1, 1)
FAR = (-2, 2, -3, 3, 4)
NEAR_ROWS = 56
FAR_ROWS = 96
COLS = 512
BF = jnp.bfloat16
F32 = jnp.float32
VMEM_LIMIT = 56 * 1024 * 1024


def params():
    return pltpu.CompilerParams(vmem_limit_bytes=VMEM_LIMIT)


def cost(flops, nbytes):
    return pl.CostEstimate(flops=flops, bytes_accessed=nbytes, transcendentals=0)


def forward_pairs():
    return [(e, (e + PLANE) % (PLANES * PLANE)) for e in range(PLANES * PLANE)]


def backward_pairs():
    return [(e, (e - PLANE) % (PLANES * PLANE)) for e in range(PLANES * PLANE)]


def after(value, *done):
    return lax.optimization_barrier((value, *done))[0]


def plane_groups():
    groups = []
    for parity in range(2):
        for core in range(2):
            for z in range(PLANES):
                groups.append(
                    [
                        ((parity ^ (j % 2)) * 2 + core) * 64 + z * PLANE + j
                        for j in range(PLANE)
                    ]
                )
    return groups


def exchange(rows, per_dest):
    sent = rows.reshape(PLANE, per_dest, D)
    got = lax.all_to_all(
        sent, ("section", "expert"), 0, 0, axis_index_groups=plane_groups(), tiled=True
    )
    return got.reshape(PLANE * per_dest, D)


def pack_body(tok_ref, routes_ref, weight_ref, out_ref):
    out_ref[0:TOK, :] = tok_ref[...]
    tail = jnp.concatenate(
        [routes_ref[...].astype(F32), weight_ref[...].astype(F32), jnp.zeros((META, COLS - 256), F32)],
        axis=1,
    )
    keep = jnp.where(pl.program_id(0) == 0, 1.0, 0.0)
    out_ref[TOK:ROWS, :] = (tail * keep).astype(BF)


def pack(tok, routes_t, weight_t):
    return pl.pallas_call(
        pack_body,
        grid=(D // COLS,),
        in_specs=[
            pl.BlockSpec((TOK, COLS), lambda i: (0, i)),
            pl.BlockSpec((META, TOK), lambda i: (0, 0)),
            pl.BlockSpec((META, TOK), lambda i: (0, 0)),
        ],
        out_specs=pl.BlockSpec((ROWS, COLS), lambda i: (0, i)),
        out_shape=jax.ShapeDtypeStruct((ROWS, D), BF),
        compiler_params=params(),
        cost_estimate=cost(0, 4 * ROWS * D),
        name="pack_rows",
    )(tok, routes_t, weight_t)


def placement(q, per_dest):
    tokens = q.shape[1]
    rows = PLANE * per_dest
    wide = jnp.broadcast_to(q[:, None, :], (PLANE, per_dest, tokens)).reshape(rows, tokens)
    code = lax.broadcasted_iota(jnp.int32, (PLANE, per_dest, tokens), 1).reshape(rows, tokens)
    return wide == code


def select_tok_body(per_dest, count, z_ref, *refs):
    blocks = refs[: len(refs) - 6]
    out_ref, q_ref, w_ref, r_ref, place, x_ref = refs[len(refs) - 6 :]
    split = count == len(FAR)
    metas = [b for b in blocks if b.shape[0] != HALF]

    @pl.when(pl.program_id(0) == 0)
    def _():
        first = z_ref[0] // PLANE * PLANE
        ids = lax.broadcasted_iota(jnp.int32, (PLANE, TOK), 0) + first
        earlier = (
            lax.broadcasted_iota(jnp.int32, (TOK, TOK), 0)
            < lax.broadcasted_iota(jnp.int32, (TOK, TOK), 1)
        ).astype(F32).astype(BF)
        for b, ref in enumerate(metas):
            base = ref.shape[0] - META
            routes = ref[base : base + META, 0:TOK].astype(F32)
            weight = ref[base : base + META, TOK : 2 * TOK].astype(F32)
            ids_f = ids.astype(F32)
            member = jnp.zeros((PLANE, TOK), F32)
            scale = jnp.zeros((PLANE, TOK), F32)
            for k in range(TOP_K):
                hit = ids_f == routes[k : k + 1, :]
                member = jnp.where(hit, 1.0, member)
                scale = jnp.where(hit, weight[k : k + 1, :], scale)
            slot = jnp.dot(member.astype(BF), earlier, preferred_element_type=F32)
            q = jnp.where(member > 0.0, slot + float(b * CAP), -1.0).astype(jnp.int32)
            q_ref[:, b * TOK : (b + 1) * TOK] = q
            w_ref[:, b * TOK : (b + 1) * TOK] = scale
            r_ref[:, b * TOK : (b + 1) * TOK] = routes
        place[...] = jnp.where(placement(q_ref[...], per_dest), 1.0, 0.0).astype(BF)

    at = 0
    for ref in blocks:
        size = HALF if split and ref.shape[0] in (HALF, HALF + META) else TOK
        x_ref[at : at + size, :] = ref[0:size, :]
        at += size
    out_ref[...] = jnp.dot(place[...], x_ref[...], preferred_element_type=F32).astype(BF)


def select_tok(z, blocks, per_dest, count):
    rows = PLANE * per_dest
    tokens = count * TOK
    const = lambda i: (0, 0)
    small = pl.BlockSpec((PLANE, tokens), const)
    return pl.pallas_call(
        functools.partial(select_tok_body, per_dest, count),
        grid=(D // COLS,),
        in_specs=[pl.BlockSpec(memory_space=pltpu.SMEM)]
        + [pl.BlockSpec((b.shape[0], COLS), lambda i: (0, i)) for b in blocks],
        out_specs=[pl.BlockSpec((rows, COLS), lambda i: (0, i)), small, small, small],
        out_shape=[
            jax.ShapeDtypeStruct((rows, D), BF),
            jax.ShapeDtypeStruct((PLANE, tokens), jnp.int32),
            jax.ShapeDtypeStruct((PLANE, tokens), F32),
            jax.ShapeDtypeStruct((PLANE, tokens), F32),
        ],
        scratch_shapes=[pltpu.VMEM((rows, tokens), BF), pltpu.VMEM((tokens, COLS), BF)],
        compiler_params=params(),
        cost_estimate=cost(2 * rows * tokens * D, 2 * D * (rows + tokens)),
        name="select_tokens",
    )(z, *blocks)


def select_cot_body(per_dest, count, q_ref, w_ref, *refs):
    blocks = refs[: len(refs) - 3]
    out_ref, place, x_ref = refs[len(refs) - 3 :]
    rows, tokens = place.shape

    @pl.when(pl.program_id(0) == 0)
    def _():
        wide = jnp.broadcast_to(w_ref[...][:, None, :], (PLANE, per_dest, tokens)).reshape(rows, tokens)
        place[...] = jnp.where(placement(q_ref[...], per_dest), wide, 0.0).astype(BF)

    at = 0
    for ref in blocks:
        size = ref.shape[0]
        x_ref[at : at + size, :] = ref[...]
        at += size
    out_ref[...] = jnp.dot(place[...], x_ref[...], preferred_element_type=F32).astype(BF)


def select_cot(q, w, blocks, per_dest, count):
    rows = PLANE * per_dest
    tokens = count * TOK
    small = pl.BlockSpec((PLANE, tokens), lambda i: (0, 0))
    return pl.pallas_call(
        functools.partial(select_cot_body, per_dest, count),
        grid=(D // COLS,),
        in_specs=[small, small]
        + [pl.BlockSpec((b.shape[0], COLS), lambda i: (0, i)) for b in blocks],
        out_specs=pl.BlockSpec((rows, COLS), lambda i: (0, i)),
        out_shape=jax.ShapeDtypeStruct((rows, D), BF),
        scratch_shapes=[pltpu.VMEM((rows, tokens), BF), pltpu.VMEM((tokens, COLS), BF)],
        compiler_params=params(),
        cost_estimate=cost(2 * rows * tokens * D, 2 * D * (rows + tokens)),
        name="select_cotangents",
    )(q, w, *blocks)


def weight_spec(which):
    return pl.BlockSpec((None, None, D, FF), lambda i: (which, 0, 0, 0))


def forward_body(x_ref, wg_ref, wu_ref, g_ref, u_ref):
    g_ref[...] = jnp.dot(x_ref[...], wg_ref[...], preferred_element_type=F32)
    u_ref[...] = jnp.dot(x_ref[...], wu_ref[...], preferred_element_type=F32)


def forward(x, weights, tile):
    rows = x.shape[0]
    out = jax.ShapeDtypeStruct((rows, FF), F32)
    spec = pl.BlockSpec((tile, FF), lambda i: (i, 0))
    return pl.pallas_call(
        forward_body,
        grid=(rows // tile,),
        in_specs=[pl.BlockSpec((tile, D), lambda i: (i, 0)), weight_spec(0), weight_spec(1)],
        out_specs=[spec, spec],
        out_shape=[out, out],
        compiler_params=params(),
        cost_estimate=cost(4 * rows * D * FF, 2 * D * (rows + 2 * FF)),
        name="expert_forward",
    )(x, weights, weights)


def backward_body(per_dest, gate_row, sc_ref, g_ref, u_ref, wg_ref, wu_ref, wd_ref,
                  rows_ref, dg_ref, du_ref, h_ref, total):
    tile = sc_ref.shape[0]
    back = jnp.dot(sc_ref[...], wd_ref[...], preferred_element_type=F32)
    gate = g_ref[...]
    up = u_ref[...]
    sig = jax.nn.sigmoid(gate)
    silu = gate * sig
    hidden = (silu * up).astype(BF)
    d_gate = (back * up * sig * (1.0 + gate * (1.0 - sig))).astype(BF)
    d_up = (back * silu).astype(BF)
    h_ref[...] = hidden
    dg_ref[...] = d_gate
    du_ref[...] = d_up
    by_ff = (((1,), (1,)), ((), ()))
    total[...] = lax.dot_general(d_gate, wg_ref[...], by_ff, preferred_element_type=F32)
    total[...] += lax.dot_general(d_up, wu_ref[...], by_ff, preferred_element_type=F32)
    product = hidden.astype(F32) * back
    ones = jnp.ones((8, FF), F32)
    pick = lax.broadcasted_iota(jnp.int32, (8, per_dest), 0) == gate_row % 8
    for d in range(tile // per_dest):
        part = lax.dot_general(
            ones, product[d * per_dest : (d + 1) * per_dest, :], by_ff,
            preferred_element_type=F32, precision=lax.Precision.HIGHEST,
        )
        at = d * per_dest + gate_row // 8 * 8
        total[at : at + 8, 0:per_dest] += jnp.where(pick, part, 0.0)
    rows_ref[...] = total[...].astype(BF)


def backward(scaled, gate, up, weights, tile, per_dest, gate_row):
    rows = scaled.shape[0]
    wide = pl.BlockSpec((tile, D), lambda i: (i, 0))
    slim = pl.BlockSpec((tile, FF), lambda i: (i, 0))
    small = jax.ShapeDtypeStruct((rows, FF), BF)
    return pl.pallas_call(
        functools.partial(backward_body, per_dest, gate_row),
        grid=(rows // tile,),
        in_specs=[wide, slim, slim, weight_spec(0), weight_spec(1), weight_spec(2)],
        out_specs=[wide, slim, slim, slim],
        out_shape=[jax.ShapeDtypeStruct((rows, D), BF), small, small, small],
        scratch_shapes=[pltpu.VMEM((tile, D), F32)],
        compiler_params=params(),
        cost_estimate=cost(6 * rows * D * FF, 4 * D * rows + 6 * D * FF),
        name="expert_backward",
    )(scaled, gate, up, weights, weights, weights)


def weight_grad_body(xn, xf, sn, sf, dgn, dgf, dun, duf, hn, hf, out_ref):
    by_rows = (((0,), (0,)), ((), ()))

    def both(a, b, c, d):
        return lax.dot_general(a[...], c[...], by_rows, preferred_element_type=F32) + lax.dot_general(
            b[...], d[...], by_rows, preferred_element_type=F32
        )

    out_ref[0] = both(xn, xf, dgn, dgf).astype(BF)
    out_ref[1] = both(xn, xf, dun, duf).astype(BF)
    out_ref[2] = both(sn, sf, hn, hf).astype(BF)


def weight_grad(near, far):
    tile = 512
    args, specs = [], []
    for a, b in zip(near, far):
        for v in (a, b):
            args.append(v)
            if v.shape[1] == D:
                specs.append(pl.BlockSpec((v.shape[0], tile), lambda i: (0, i)))
            else:
                specs.append(pl.BlockSpec(v.shape, lambda i: (0, 0)))
    rows = near[0].shape[0] + far[0].shape[0]
    return pl.pallas_call(
        weight_grad_body,
        grid=(D // tile,),
        in_specs=specs,
        out_specs=pl.BlockSpec((3, None, tile, FF), lambda i: (0, 0, i, 0)),
        out_shape=jax.ShapeDtypeStruct((3, 1, D, FF), BF),
        compiler_params=params(),
        cost_estimate=cost(6 * rows * D * FF, 4 * rows * D + 6 * D * FF),
        name="weight_grads",
    )(*args)


def combine_body(per_dest, count, gate_row, z_ref, q_ref, w_ref, r_ref, x_ref, *refs):
    place = refs[-1]
    outs = refs[:-1]
    rows, tokens = place.shape
    first_step = pl.program_id(0) == 0

    @pl.when(first_step)
    def _():
        place[...] = jnp.where(placement(q_ref[...], per_dest), 1.0, 0.0).astype(BF)

    summed = lax.dot_general(
        place[...], x_ref[...], (((0,), (0,)), ((), ())), preferred_element_type=F32
    ).astype(BF)
    at = 0
    for ref in outs:
        size = ref.shape[0] if ref.shape[0] == HALF else ref.shape[0] - META
        ref[0:size, :] = summed[at : at + size, :]
        if ref.shape[0] != HALF:
            ref[size : size + META, :] = jnp.zeros((META, COLS), BF)
        at += size

    @pl.when(first_step)
    def _():
        first = z_ref[0] // PLANE * PLANE
        find = (
            lax.broadcasted_iota(jnp.int32, (PLANE, rows), 1)
            == lax.broadcasted_iota(jnp.int32, (PLANE, rows), 0) * per_dest + gate_row
        )
        gates = jnp.dot(
            jnp.where(find, 1.0, 0.0).astype(BF), x_ref[:, 0:TOK], preferred_element_type=F32
        )
        by_code = jnp.zeros((PLANE, tokens), F32)
        line = lax.broadcasted_iota(jnp.int32, (PLANE, TOK), 0)
        lane = lax.broadcasted_iota(jnp.int32, (PLANE, TOK), 1)
        code = lax.broadcasted_iota(jnp.int32, (TOK, tokens), 0)
        for j in range(PLANE):
            own = jnp.where((line == j) & (lane < count * CAP), gates, 0.0).astype(BF)
            hit = jnp.where(code == q_ref[j : j + 1, :], 1.0, 0.0).astype(BF)
            by_code = by_code + jnp.dot(own, hit, preferred_element_type=F32)
        weight = w_ref[...]
        by_code = jnp.where(weight > 0.0, by_code / jnp.where(weight > 0.0, weight, 1.0), 0.0)
        routes = r_ref[...]
        by_k = jnp.zeros((PLANE, tokens), F32)
        for j in range(PLANE):
            mine = routes == (first + j).astype(F32)
            by_k = jnp.where(mine, by_code[j : j + 1, :], by_k)
        b = 0
        for ref in outs:
            if ref.shape[0] == HALF:
                continue
            size = ref.shape[0] - META
            ref[size : size + META, 0:TOK] = by_k[:, b * TOK : (b + 1) * TOK].astype(BF)
            b += 1


def combine(z, q, w, r, x, sizes, per_dest, count, gate_row):
    rows = PLANE * per_dest
    tokens = count * TOK
    small = pl.BlockSpec((PLANE, tokens), lambda i: (0, 0))
    return pl.pallas_call(
        functools.partial(combine_body, per_dest, count, gate_row),
        grid=(D // COLS,),
        in_specs=[
            pl.BlockSpec(memory_space=pltpu.SMEM),
            small,
            small,
            small,
            pl.BlockSpec((rows, COLS), lambda i: (0, i)),
        ],
        out_specs=[pl.BlockSpec((n, COLS), lambda i: (0, i)) for n in sizes],
        out_shape=[jax.ShapeDtypeStruct((n, D), BF) for n in sizes],
        scratch_shapes=[pltpu.VMEM((rows, tokens), BF)],
        compiler_params=params(),
        cost_estimate=cost(2 * rows * tokens * D, 2 * D * (rows + tokens)),
        name="combine_rows",
    )(z, q, w, r, x)


def ring_gather(own):
    fw, bw = forward_pairs(), backward_pairs()
    got = {0: own}
    down = up = own
    for step in (1, 2, 3):
        down = lax.ppermute(down, "expert", fw)
        up = lax.ppermute(up, "expert", bw)
        got[-step], got[step] = down, up
    top = lax.ppermute(down[:HALF], "expert", fw)
    low = lax.ppermute(up[HALF:], "expert", bw)
    near = [got[k] for k in NEAR]
    far = [got[k] for k in FAR[:-1]] + [top, low]
    return near, far


def added(a, b):
    return (a.astype(F32) + b.astype(F32)).astype(BF)


def ring_scatter(near, far):
    fw, bw = forward_pairs(), backward_pairs()
    part = dict(zip(NEAR, near)) | dict(zip(FAR[:-1], far[:-2]))
    top = lax.ppermute(far[-2], "expert", fw)
    low = lax.ppermute(far[-1], "expert", bw)
    ahead = added(part[3], jnp.pad(top, ((0, META + HALF), (0, 0))))
    behind = added(part[-3], jnp.pad(low, ((HALF, 0), (0, 0))))
    for step in (2, 1):
        ahead = added(part[step], lax.ppermute(ahead, "expert", fw))
        behind = added(part[-step], lax.ppermute(behind, "expert", bw))
    ahead = lax.ppermute(ahead, "expert", fw)
    behind = lax.ppermute(behind, "expert", bw)
    return part[0].astype(F32) + ahead.astype(F32) + behind.astype(F32)


def per_device(tokens, cotangent, routes, route_weights, weights):
    z = lax.axis_index("expert").reshape(1).astype(jnp.int32)
    own = pack(tokens[0], routes[0].T, route_weights[0].T)
    tok_near, tok_far = ring_gather(own)
    cot_near, cot_far = ring_gather(after(cotangent[0], tok_far[-1], tok_far[-2]))

    send_near, qn, wn, rn = select_tok(z, tok_near, NEAR_ROWS, len(NEAR))
    xn = exchange(send_near, NEAR_ROWS)
    send_far, qf, wf, rf = select_tok(z, tok_far, FAR_ROWS, len(FAR))
    xf = exchange(send_far, FAR_ROWS)
    sn = exchange(select_cot(qn, wn, cot_near, NEAR_ROWS, len(NEAR)), NEAR_ROWS)
    sf = exchange(select_cot(qf, wf, cot_far, FAR_ROWS, len(FAR)), FAR_ROWS)

    tile_n, tile_f = 4 * NEAR_ROWS, 2 * FAR_ROWS
    gn, un = forward(xn, weights, tile_n)
    gf, uf = forward(xf, weights, tile_f)
    near_gate, far_gate = len(NEAR) * CAP, len(FAR) * CAP
    rows_n, dgn, dun, hn = backward(sn, gn, un, weights, tile_n, NEAR_ROWS, near_gate)
    rows_f, dgf, duf, hf = backward(sf, gf, uf, weights, tile_f, FAR_ROWS, far_gate)
    back_f = exchange(rows_f, FAR_ROWS)
    back_n = exchange(rows_n, NEAR_ROWS)

    part = weight_grad((xn, sn, dgn, dun, after(hn, back_f)), (xf, sf, dgf, duf, hf))
    summed = lax.psum_scatter(part, "section", scatter_dimension=2, tiled=True)
    weight_grads = summed.astype(F32) / lax.axis_size("section")

    far_sizes = [ROWS] * 4 + [HALF, HALF + META]
    far_parts = combine(z, qf, wf, rf, back_f, far_sizes, FAR_ROWS, len(FAR), far_gate)
    near_parts = combine(z, qn, wn, rn, back_n, [ROWS] * 3, NEAR_ROWS, len(NEAR), near_gate)
    total = ring_scatter(near_parts, far_parts)
    token_grads = total[:TOK].astype(BF)[None]
    gate_grads = total[TOK:, :TOK].T.astype(BF)[None]
    return token_grads, gate_grads, weight_grads


def solution(mesh):
    placed = (
        P("section", "expert", None),
        P("section", "expert", None),
        P("section", "expert", None),
        P("section", "expert", None),
        P(None, "expert", None, None),
    )
    return jax.shard_map(
        per_device,
        mesh=mesh,
        in_specs=placed,
        out_specs=(
            P("section", "expert", None),
            P("section", "expert", None),
            P(None, "expert", "section", None),
        ),
        check_vma=False,
    )
```

```python
import functools

import jax
import jax.numpy as jnp
from jax import lax
from jax.experimental import pallas as pl
from jax.experimental.pallas import tpu as pltpu
from jax.sharding import PartitionSpec as P

D = 2048
FF = 384
TOP_K = 8
TOK = 128
CAP = 18
PLANES = 8
PLANE = 8
META = 8
ROWS = TOK + META
HALF = 64
NEAR = (0, -1, 1)
FAR = (-2, 2, -3, 3, 4)
NEAR_ROWS = 56
FAR_ROWS = 96
COLS = 1024
BF = jnp.bfloat16
F32 = jnp.float32
VMEM_LIMIT = 32 * 1024 * 1024


def params():
    return pltpu.CompilerParams(vmem_limit_bytes=VMEM_LIMIT)


def cost(flops, nbytes):
    return pl.CostEstimate(flops=flops, bytes_accessed=nbytes, transcendentals=0)


def forward_pairs():
    return [(e, (e + PLANE) % (PLANES * PLANE)) for e in range(PLANES * PLANE)]


def backward_pairs():
    return [(e, (e - PLANE) % (PLANES * PLANE)) for e in range(PLANES * PLANE)]


def ordered(*values):
    return lax.optimization_barrier(values)


def plane_groups():
    groups = []
    for parity in range(2):
        for core in range(2):
            for z in range(PLANES):
                groups.append(
                    [
                        ((parity ^ (j % 2)) * 2 + core) * 64 + z * PLANE + j
                        for j in range(PLANE)
                    ]
                )
    return groups


def exchange(rows, per_dest):
    sent = rows.reshape(PLANE, per_dest, D)
    got = lax.all_to_all(
        sent, ("section", "expert"), 0, 0, axis_index_groups=plane_groups(), tiled=True
    )
    return got.reshape(PLANE * per_dest, D)


def pack_body(tok_ref, routes_ref, weight_ref, out_ref):
    out_ref[0:TOK, :] = tok_ref[...]
    out_ref[TOK:ROWS, :] = jnp.concatenate(
        [routes_ref[...].astype(F32), weight_ref[...].astype(F32), jnp.zeros((META, D - 2 * TOK), F32)],
        axis=1,
    ).astype(BF)


def pack(tok, routes_t, weight_t):
    return pl.pallas_call(
        pack_body,
        out_shape=jax.ShapeDtypeStruct((ROWS, D), BF),
        compiler_params=params(),
        cost_estimate=cost(0, 4 * ROWS * D),
        name="pack_rows",
    )(tok, routes_t, weight_t)


def placement(q, per_dest):
    tokens = q.shape[1]
    rows = PLANE * per_dest
    wide = jnp.broadcast_to(q[:, None, :], (PLANE, per_dest, tokens)).reshape(rows, tokens)
    code = lax.broadcasted_iota(jnp.int32, (PLANE, per_dest, tokens), 1).reshape(rows, tokens)
    return wide == code


def select_tok_body(per_dest, count, z_ref, *refs):
    blocks = refs[: len(refs) - 6]
    out_ref, q_ref, w_ref, r_ref, place, x_ref = refs[len(refs) - 6 :]
    split = count == len(FAR)
    metas = [b for b in blocks if b.shape[0] != HALF]

    @pl.when(pl.program_id(0) == 0)
    def _():
        first = z_ref[0] // PLANE * PLANE
        ids = lax.broadcasted_iota(jnp.int32, (PLANE, TOK), 0) + first
        earlier = (
            lax.broadcasted_iota(jnp.int32, (TOK, TOK), 0)
            < lax.broadcasted_iota(jnp.int32, (TOK, TOK), 1)
        ).astype(F32).astype(BF)
        for b, ref in enumerate(metas):
            base = ref.shape[0] - META
            routes = ref[base : base + META, 0:TOK].astype(F32)
            weight = ref[base : base + META, TOK : 2 * TOK].astype(F32)
            ids_f = ids.astype(F32)
            member = jnp.zeros((PLANE, TOK), F32)
            scale = jnp.zeros((PLANE, TOK), F32)
            for k in range(TOP_K):
                hit = ids_f == routes[k : k + 1, :]
                member = jnp.where(hit, 1.0, member)
                scale = jnp.where(hit, weight[k : k + 1, :], scale)
            slot = jnp.dot(member.astype(BF), earlier, preferred_element_type=F32)
            q = jnp.where(member > 0.0, slot + float(b * CAP), -1.0).astype(jnp.int32)
            q_ref[:, b * TOK : (b + 1) * TOK] = q
            w_ref[:, b * TOK : (b + 1) * TOK] = scale
            r_ref[:, b * TOK : (b + 1) * TOK] = routes
        place[...] = jnp.where(placement(q_ref[...], per_dest), 1.0, 0.0).astype(BF)

    at = 0
    for ref in blocks:
        size = HALF if split and ref.shape[0] in (HALF, HALF + META) else TOK
        x_ref[at : at + size, :] = ref[0:size, :]
        at += size
    out_ref[...] = jnp.dot(place[...], x_ref[...], preferred_element_type=F32).astype(BF)


def select_tok(z, blocks, per_dest, count):
    rows = PLANE * per_dest
    tokens = count * TOK
    const = lambda i: (0, 0)
    small = pl.BlockSpec((PLANE, tokens), const)
    return pl.pallas_call(
        functools.partial(select_tok_body, per_dest, count),
        grid=(D // COLS,),
        in_specs=[pl.BlockSpec(memory_space=pltpu.SMEM)]
        + [pl.BlockSpec((b.shape[0], COLS), lambda i: (0, i)) for b in blocks],
        out_specs=[pl.BlockSpec((rows, COLS), lambda i: (0, i)), small, small, small],
        out_shape=[
            jax.ShapeDtypeStruct((rows, D), BF),
            jax.ShapeDtypeStruct((PLANE, tokens), jnp.int32),
            jax.ShapeDtypeStruct((PLANE, tokens), F32),
            jax.ShapeDtypeStruct((PLANE, tokens), F32),
        ],
        scratch_shapes=[pltpu.VMEM((rows, tokens), BF), pltpu.VMEM((tokens, COLS), BF)],
        compiler_params=params(),
        cost_estimate=cost(2 * rows * tokens * D, 2 * D * (rows + tokens)),
        name="select_tokens",
    )(z, *blocks)


def select_cot_body(per_dest, count, q_ref, w_ref, *refs):
    blocks = refs[: len(refs) - 3]
    out_ref, place, x_ref = refs[len(refs) - 3 :]
    rows, tokens = place.shape

    @pl.when(pl.program_id(0) == 0)
    def _():
        wide = jnp.broadcast_to(w_ref[...][:, None, :], (PLANE, per_dest, tokens)).reshape(rows, tokens)
        place[...] = jnp.where(placement(q_ref[...], per_dest), wide, 0.0).astype(BF)

    at = 0
    for ref in blocks:
        size = ref.shape[0]
        x_ref[at : at + size, :] = ref[...]
        at += size
    out_ref[...] = jnp.dot(place[...], x_ref[...], preferred_element_type=F32).astype(BF)


def select_cot(q, w, blocks, per_dest, count):
    rows = PLANE * per_dest
    tokens = count * TOK
    small = pl.BlockSpec((PLANE, tokens), lambda i: (0, 0))
    return pl.pallas_call(
        functools.partial(select_cot_body, per_dest, count),
        grid=(D // COLS,),
        in_specs=[small, small]
        + [pl.BlockSpec((b.shape[0], COLS), lambda i: (0, i)) for b in blocks],
        out_specs=pl.BlockSpec((rows, COLS), lambda i: (0, i)),
        out_shape=jax.ShapeDtypeStruct((rows, D), BF),
        scratch_shapes=[pltpu.VMEM((rows, tokens), BF), pltpu.VMEM((tokens, COLS), BF)],
        compiler_params=params(),
        cost_estimate=cost(2 * rows * tokens * D, 2 * D * (rows + tokens)),
        name="select_cotangents",
    )(q, w, *blocks)


def resident():
    return pl.BlockSpec(memory_space=pltpu.VMEM)


def join_body(g_ref, u_ref, d_ref, out_ref, down_ref):
    out_ref[:, 0:FF] = g_ref[...]
    out_ref[:, FF : 2 * FF] = u_ref[...]
    down_ref[...] = d_ref[...]


def join_weights(weights):
    rows = D // 2

    def part(which):
        return pl.BlockSpec((None, None, rows, FF), lambda i: (which, 0, i, 0))

    return pl.pallas_call(
        join_body,
        grid=(2,),
        in_specs=[part(0), part(1), part(2)],
        out_specs=[
            pl.BlockSpec((rows, 2 * FF), lambda i: (i, 0)),
            pl.BlockSpec((rows, FF), lambda i: (i, 0)),
        ],
        out_shape=[jax.ShapeDtypeStruct((D, 2 * FF), BF), jax.ShapeDtypeStruct((D, FF), BF)],
        compiler_params=params(),
        cost_estimate=cost(0, 12 * D * FF),
        name="join_weights",
    )(weights, weights, weights)


def forward_body(x_ref, w_ref, p_ref):
    p_ref[...] = jnp.dot(x_ref[...], w_ref[...], preferred_element_type=F32)


def forward(x, joined, tile):
    rows = x.shape[0]
    return pl.pallas_call(
        forward_body,
        grid=(rows // tile,),
        in_specs=[pl.BlockSpec((tile, D), lambda i: (i, 0)), resident()],
        out_specs=pl.BlockSpec((tile, 2 * FF), lambda i: (i, 0)),
        out_shape=jax.ShapeDtypeStruct((rows, 2 * FF), F32),
        compiler_params=params(),
        cost_estimate=cost(4 * rows * D * FF, 2 * D * (rows + 2 * FF)),
        name="expert_forward",
    )(x, joined)


def backward_body(per_dest, gate_row, sc_ref, p_ref, w_ref, wd_ref, rows_ref, d_ref, h_ref):
    tile = sc_ref.shape[0]
    back = jnp.dot(sc_ref[...], wd_ref[...], preferred_element_type=F32)
    gate = p_ref[:, 0:FF]
    up = p_ref[:, FF : 2 * FF]
    sig = jax.nn.sigmoid(gate)
    silu = gate * sig
    hidden = (silu * up).astype(BF)
    d_gate = (back * up * sig * (1.0 + gate * (1.0 - sig))).astype(BF)
    d_up = (back * silu).astype(BF)
    h_ref[...] = hidden
    d_ref[:, 0:FF] = d_gate
    d_ref[:, FF : 2 * FF] = d_up
    by_ff = (((1,), (1,)), ((), ()))
    rows_ref[...] = lax.dot_general(d_ref[...], w_ref[...], by_ff, preferred_element_type=F32).astype(BF)
    product = hidden.astype(F32) * back
    high = product.astype(BF)
    low = (product - high.astype(F32)).astype(BF)
    ones = jnp.ones((16, FF), BF)
    line = lax.broadcasted_iota(jnp.int32, (16, per_dest), 0)
    for d in range(tile // per_dest):
        own = slice(d * per_dest, (d + 1) * per_dest)
        part = lax.dot_general(ones, high[own], by_ff, preferred_element_type=F32)
        part += lax.dot_general(ones, low[own], by_ff, preferred_element_type=F32)
        row = d * per_dest + gate_row
        at = row // 16 * 16
        window = rows_ref[at : at + 16, 0:per_dest].astype(F32)
        rows_ref[at : at + 16, 0:per_dest] = jnp.where(line == row - at, part, window).astype(BF)


def backward(scaled, pre, joined, down, tile, per_dest, gate_row):
    rows = scaled.shape[0]
    wide = pl.BlockSpec((tile, D), lambda i: (i, 0))
    slim = pl.BlockSpec((tile, FF), lambda i: (i, 0))
    return pl.pallas_call(
        functools.partial(backward_body, per_dest, gate_row),
        grid=(rows // tile,),
        in_specs=[
            wide,
            pl.BlockSpec((tile, 2 * FF), lambda i: (i, 0)),
            resident(),
            resident(),
        ],
        out_specs=[wide, pl.BlockSpec((tile, 2 * FF), lambda i: (i, 0)), slim],
        out_shape=[
            jax.ShapeDtypeStruct((rows, D), BF),
            jax.ShapeDtypeStruct((rows, 2 * FF), BF),
            jax.ShapeDtypeStruct((rows, FF), BF),
        ],
        compiler_params=params(),
        cost_estimate=cost(6 * rows * D * FF, 4 * D * rows + 6 * D * FF),
        name="expert_backward",
    )(scaled, pre, joined, down)


def weight_grad_body(sec_ref, xn, xf, sn, sf, dn, df, hn, hf, sent_ref, kept_ref):
    by_rows = (((0,), (0,)), ((), ()))

    def both(a, b, c, d):
        return (
            lax.dot_general(a[...], c[...], by_rows, preferred_element_type=F32)
            + lax.dot_general(b[...], d[...], by_rows, preferred_element_type=F32)
        ).astype(BF)

    inner = both(xn, xf, dn, df)
    outer = both(sn, sf, hn, hf)

    def store(ref):
        ref[0] = inner[:, 0:FF]
        ref[1] = inner[:, FF : 2 * FF]
        ref[2] = outer

    pl.when(pl.program_id(0) < 2)(lambda: store(sent_ref))
    pl.when(pl.program_id(0) >= 2)(lambda: store(kept_ref))


def weight_grad(section, near, far):
    tile = D // 4
    args, specs = [], []
    for a, b in zip(near, far):
        for v in (a, b):
            args.append(v)
            if v.shape[1] == D:
                specs.append(
                    pl.BlockSpec(
                        (v.shape[0], tile), lambda i, sec: (0, sec[0] ^ (2 * i + 1 - 5 * (i // 2)))
                    )
                )
            else:
                specs.append(pl.BlockSpec(v.shape, lambda i, sec: (0, 0)))
    rows = near[0].shape[0] + far[0].shape[0]
    out = jax.ShapeDtypeStruct((2, 3, tile, FF), BF)
    return pl.pallas_call(
        weight_grad_body,
        grid_spec=pltpu.PrefetchScalarGridSpec(
            num_scalar_prefetch=1,
            grid=(4,),
            in_specs=specs,
            out_specs=[
                pl.BlockSpec((None, 3, tile, FF), lambda i, sec: (jnp.minimum(i, 1), 0, 0, 0)),
                pl.BlockSpec((None, 3, tile, FF), lambda i, sec: (jnp.maximum(i - 2, 0), 0, 0, 0)),
            ],
        ),
        out_shape=[out, out],
        compiler_params=params(),
        cost_estimate=cost(6 * rows * D * FF, 4 * rows * D + 6 * D * FF),
        name="weight_grads",
    )(section, *args)


def section_mean(sent, kept):
    other_core = [(s, s ^ 1) for s in range(4)]
    other_chip = [(s, s ^ 2) for s in range(4)]
    got = lax.ppermute(sent, "section", other_core)
    onward = added(kept[1], got[1])
    last = lax.ppermute(onward, "section", other_chip)
    total = kept[0].astype(F32) + got[0].astype(F32) + last.astype(F32)
    return (total / 4.0)[:, None]


def combine_body(per_dest, count, gate_row, z_ref, q_ref, w_ref, r_ref, x_ref, *refs):
    place = refs[-1]
    outs = refs[:-1]
    rows, tokens = place.shape
    first_step = pl.program_id(0) == 0

    @pl.when(first_step)
    def _():
        place[...] = jnp.where(placement(q_ref[...], per_dest), 1.0, 0.0).astype(BF)

    summed = lax.dot_general(
        place[...], x_ref[...], (((0,), (0,)), ((), ())), preferred_element_type=F32
    ).astype(BF)
    at = 0
    for ref in outs:
        size = ref.shape[0] if ref.shape[0] == HALF else ref.shape[0] - META
        ref[0:size, :] = summed[at : at + size, :]
        if ref.shape[0] != HALF:
            ref[size : size + META, :] = jnp.zeros((META, COLS), BF)
        at += size

    @pl.when(first_step)
    def _():
        first = z_ref[0] // PLANE * PLANE
        find = (
            lax.broadcasted_iota(jnp.int32, (PLANE, rows), 1)
            == lax.broadcasted_iota(jnp.int32, (PLANE, rows), 0) * per_dest + gate_row
        )
        gates = jnp.dot(
            jnp.where(find, 1.0, 0.0).astype(BF), x_ref[:, 0:TOK], preferred_element_type=F32
        )
        by_code = jnp.zeros((PLANE, tokens), F32)
        line = lax.broadcasted_iota(jnp.int32, (PLANE, TOK), 0)
        lane = lax.broadcasted_iota(jnp.int32, (PLANE, TOK), 1)
        code = lax.broadcasted_iota(jnp.int32, (TOK, tokens), 0)
        for j in range(PLANE):
            own = jnp.where((line == j) & (lane < count * CAP), gates, 0.0).astype(BF)
            hit = jnp.where(code == q_ref[j : j + 1, :], 1.0, 0.0).astype(BF)
            by_code = by_code + jnp.dot(own, hit, preferred_element_type=F32)
        weight = w_ref[...]
        by_code = jnp.where(weight > 0.0, by_code / jnp.where(weight > 0.0, weight, 1.0), 0.0)
        routes = r_ref[...]
        by_k = jnp.zeros((PLANE, tokens), F32)
        for j in range(PLANE):
            mine = routes == (first + j).astype(F32)
            by_k = jnp.where(mine, by_code[j : j + 1, :], by_k)
        b = 0
        for ref in outs:
            if ref.shape[0] == HALF:
                continue
            size = ref.shape[0] - META
            ref[size : size + META, 0:TOK] = by_k[:, b * TOK : (b + 1) * TOK].astype(BF)
            b += 1


def combine(z, q, w, r, x, sizes, per_dest, count, gate_row):
    rows = PLANE * per_dest
    tokens = count * TOK
    small = pl.BlockSpec((PLANE, tokens), lambda i: (0, 0))
    return pl.pallas_call(
        functools.partial(combine_body, per_dest, count, gate_row),
        grid=(D // COLS,),
        in_specs=[
            pl.BlockSpec(memory_space=pltpu.SMEM),
            small,
            small,
            small,
            pl.BlockSpec((rows, COLS), lambda i: (0, i)),
        ],
        out_specs=[pl.BlockSpec((n, COLS), lambda i: (0, i)) for n in sizes],
        out_shape=[jax.ShapeDtypeStruct((n, D), BF) for n in sizes],
        scratch_shapes=[pltpu.VMEM((rows, tokens), BF)],
        compiler_params=params(),
        cost_estimate=cost(2 * rows * tokens * D, 2 * D * (rows + tokens)),
        name="combine_rows",
    )(z, q, w, r, x)


def ring_gather(own):
    fw, bw = forward_pairs(), backward_pairs()
    got = {0: own}
    down = up = own
    for step in (1, 2, 3):
        down = lax.ppermute(down, "expert", fw)
        up = lax.ppermute(up, "expert", bw)
        got[-step], got[step] = down, up
    top = lax.ppermute(down[:HALF], "expert", fw)
    low = lax.ppermute(up[HALF:], "expert", bw)
    near = [got[k] for k in NEAR]
    far = [got[k] for k in FAR[:-1]] + [top, low]
    return near, far


def added(a, b):
    return (a.astype(F32) + b.astype(F32)).astype(BF)


def ring_scatter(near, far):
    fw, bw = forward_pairs(), backward_pairs()
    part = dict(zip(NEAR, near)) | dict(zip(FAR[:-1], far[:-2]))
    top = lax.ppermute(far[-2], "expert", fw)
    low = lax.ppermute(far[-1], "expert", bw)
    ahead = added(part[3], jnp.pad(top, ((0, META + HALF), (0, 0))))
    behind = added(part[-3], jnp.pad(low, ((HALF, 0), (0, 0))))
    for step in (2, 1):
        ahead = added(part[step], lax.ppermute(ahead, "expert", fw))
        behind = added(part[-step], lax.ppermute(behind, "expert", bw))
    ahead = lax.ppermute(ahead, "expert", fw)
    behind = lax.ppermute(behind, "expert", bw)
    return part[0].astype(F32) + ahead.astype(F32) + behind.astype(F32)


def per_device(tokens, cotangent, routes, route_weights, weights):
    z = lax.axis_index("expert").reshape(1).astype(jnp.int32)
    section = lax.axis_index("section").reshape(1).astype(jnp.int32)
    own = pack(tokens[0], routes[0].T, route_weights[0].T)
    tok_near, tok_far = ring_gather(own)
    joined, down = join_weights(weights)
    cot, tok_near[1], tok_near[2] = ordered(cotangent[0], tok_near[1], tok_near[2])
    cot_near, cot_far = ring_gather(cot)

    send, qn, wn, rn = select_tok(z, tok_near, NEAR_ROWS, len(NEAR))
    xn = exchange(send, NEAR_ROWS)
    send = select_cot(qn, wn, cot_near, NEAR_ROWS, len(NEAR))
    send, xn, tok_far[0], tok_far[1] = ordered(send, xn, tok_far[0], tok_far[1])
    sn = exchange(send, NEAR_ROWS)
    send, qf, wf, rf = select_tok(z, tok_far, FAR_ROWS, len(FAR))
    send, sn = ordered(send, sn)
    xf = exchange(send, FAR_ROWS)
    send, xf = ordered(select_cot(qf, wf, cot_far, FAR_ROWS, len(FAR)), xf)
    sf = exchange(send, FAR_ROWS)

    near_tile, far_tile = 4 * NEAR_ROWS, 4 * FAR_ROWS
    pn = forward(xn, joined, near_tile)
    pf = forward(xf, joined, far_tile)
    near_gate, far_gate = len(NEAR) * CAP, len(FAR) * CAP
    rows_n, dn, hn = backward(sn, pn, joined, down, near_tile, NEAR_ROWS, near_gate)
    sf, rows_n, pf = ordered(sf, rows_n, pf)
    rows_f, df, hf = backward(sf, pf, joined, down, far_tile, FAR_ROWS, far_gate)
    back_f = exchange(rows_f, FAR_ROWS)
    rows_n, back_f = ordered(rows_n, back_f)
    back_n = exchange(rows_n, NEAR_ROWS)

    sent, kept = weight_grad(section, (xn, sn, dn, hn), (xf, sf, df, hf))
    far_sizes = [ROWS] * 4 + [HALF, HALF + META]
    far_parts = combine(z, qf, wf, rf, back_f, far_sizes, FAR_ROWS, len(FAR), far_gate)
    near_parts = combine(z, qn, wn, rn, back_n, [ROWS] * 3, NEAR_ROWS, len(NEAR), near_gate)
    total = ring_scatter(near_parts, far_parts)
    token_grads = total[:TOK].astype(BF)[None]
    gate_grads = total[TOK:, :TOK].T.astype(BF)[None]
    return token_grads, gate_grads, section_mean(sent, kept)


def solution(mesh):
    placed = (
        P("section", "expert", None),
        P("section", "expert", None),
        P("section", "expert", None),
        P("section", "expert", None),
        P(None, "expert", None, None),
    )
    return jax.shard_map(
        per_device,
        mesh=mesh,
        in_specs=placed,
        out_specs=(
            P("section", "expert", None),
            P("section", "expert", None),
            P(None, "expert", "section", None),
        ),
        check_vma=False,
    )
```

```python
import functools

import jax
import jax.numpy as jnp
from jax import lax
from jax.experimental import pallas as pl
from jax.experimental.pallas import tpu as pltpu
from jax.sharding import PartitionSpec as P

D = 2048
FF = 384
TOP_K = 8
TOK = 128
CAP = 18
PLANES = 8
PLANE = 8
META = 8
ROWS = TOK + META
HALF = 64
NEAR = (0, -1, 1)
FAR = (-2, 2, -3, 3, 4)
NEAR_ROWS = 56
FAR_ROWS = 96
COLS = 1024
BF = jnp.bfloat16
F32 = jnp.float32
VMEM_LIMIT = 32 * 1024 * 1024


def params():
    return pltpu.CompilerParams(vmem_limit_bytes=VMEM_LIMIT)


def cost(flops, nbytes):
    return pl.CostEstimate(flops=flops, bytes_accessed=nbytes, transcendentals=0)


def far_memory(shape, dtype=BF):
    return pltpu.HBM(shape, dtype)


def pinned(*arrays):
    return [pltpu.with_memory_space_constraint(a, pltpu.HBM) for a in arrays]


def forward_pairs():
    return [(e, (e + PLANE) % (PLANES * PLANE)) for e in range(PLANES * PLANE)]


def backward_pairs():
    return [(e, (e - PLANE) % (PLANES * PLANE)) for e in range(PLANES * PLANE)]


def ordered(*values):
    return lax.optimization_barrier(values)


def plane_groups():
    groups = []
    for parity in range(2):
        for core in range(2):
            for z in range(PLANES):
                groups.append(
                    [
                        ((parity ^ (j % 2)) * 2 + core) * 64 + z * PLANE + j
                        for j in range(PLANE)
                    ]
                )
    return groups


def exchange(rows, per_dest):
    sent = rows.reshape(PLANE, per_dest, D)
    got = lax.all_to_all(
        sent, ("section", "expert"), 0, 0, axis_index_groups=plane_groups(), tiled=True
    )
    return got.reshape(PLANE * per_dest, D)


def pack_body(tok_ref, routes_ref, weight_ref, out_ref):
    out_ref[0:TOK, :] = tok_ref[...]
    out_ref[TOK:ROWS, :] = jnp.concatenate(
        [routes_ref[...].astype(F32), weight_ref[...].astype(F32), jnp.zeros((META, D - 2 * TOK), F32)],
        axis=1,
    ).astype(BF)


def pack(tok, routes_t, weight_t):
    return pl.pallas_call(
        pack_body,
        out_shape=jax.ShapeDtypeStruct((ROWS, D), BF),
        compiler_params=params(),
        cost_estimate=cost(0, 4 * ROWS * D),
        name="pack_rows",
    )(tok, routes_t, weight_t)


def placement(q, per_dest):
    tokens = q.shape[1]
    rows = PLANE * per_dest
    wide = jnp.broadcast_to(q[:, None, :], (PLANE, per_dest, tokens)).reshape(rows, tokens)
    code = lax.broadcasted_iota(jnp.int32, (PLANE, per_dest, tokens), 1).reshape(rows, tokens)
    return wide == code


def select_tok_body(per_dest, count, z_ref, *refs):
    blocks = refs[: len(refs) - 6]
    out_ref, q_ref, w_ref, r_ref, place, x_ref = refs[len(refs) - 6 :]
    split = count == len(FAR)
    metas = [b for b in blocks if b.shape[0] != HALF]

    @pl.when(pl.program_id(0) == 0)
    def _():
        first = z_ref[0] // PLANE * PLANE
        ids = lax.broadcasted_iota(jnp.int32, (PLANE, TOK), 0) + first
        earlier = (
            lax.broadcasted_iota(jnp.int32, (TOK, TOK), 0)
            < lax.broadcasted_iota(jnp.int32, (TOK, TOK), 1)
        ).astype(F32).astype(BF)
        for b, ref in enumerate(metas):
            base = ref.shape[0] - META
            routes = ref[base : base + META, 0:TOK].astype(F32)
            weight = ref[base : base + META, TOK : 2 * TOK].astype(F32)
            ids_f = ids.astype(F32)
            member = jnp.zeros((PLANE, TOK), F32)
            scale = jnp.zeros((PLANE, TOK), F32)
            for k in range(TOP_K):
                hit = ids_f == routes[k : k + 1, :]
                member = jnp.where(hit, 1.0, member)
                scale = jnp.where(hit, weight[k : k + 1, :], scale)
            slot = jnp.dot(member.astype(BF), earlier, preferred_element_type=F32)
            q = jnp.where(member > 0.0, slot + float(b * CAP), -1.0).astype(jnp.int32)
            q_ref[:, b * TOK : (b + 1) * TOK] = q
            w_ref[:, b * TOK : (b + 1) * TOK] = scale
            r_ref[:, b * TOK : (b + 1) * TOK] = routes
        place[...] = jnp.where(placement(q_ref[...], per_dest), 1.0, 0.0).astype(BF)

    at = 0
    for ref in blocks:
        size = HALF if split and ref.shape[0] in (HALF, HALF + META) else TOK
        x_ref[at : at + size, :] = ref[0:size, :]
        at += size
    out_ref[...] = jnp.dot(place[...], x_ref[...], preferred_element_type=F32).astype(BF)


def select_tok(z, blocks, per_dest, count):
    rows = PLANE * per_dest
    tokens = count * TOK
    const = lambda i: (0, 0)
    small = pl.BlockSpec((PLANE, tokens), const)
    return pl.pallas_call(
        functools.partial(select_tok_body, per_dest, count),
        grid=(D // COLS,),
        in_specs=[pl.BlockSpec(memory_space=pltpu.SMEM)]
        + [pl.BlockSpec((b.shape[0], COLS), lambda i: (0, i)) for b in blocks],
        out_specs=[pl.BlockSpec((rows, COLS), lambda i: (0, i)), small, small, small],
        out_shape=[
            far_memory((rows, D)),
            jax.ShapeDtypeStruct((PLANE, tokens), jnp.int32),
            jax.ShapeDtypeStruct((PLANE, tokens), F32),
            jax.ShapeDtypeStruct((PLANE, tokens), F32),
        ],
        scratch_shapes=[pltpu.VMEM((rows, tokens), BF), pltpu.VMEM((tokens, COLS), BF)],
        compiler_params=params(),
        cost_estimate=cost(2 * rows * tokens * D, 2 * D * (rows + tokens)),
        name="select_tokens",
    )(z, *blocks)


def select_cot_body(per_dest, count, q_ref, w_ref, *refs):
    blocks = refs[: len(refs) - 3]
    out_ref, place, x_ref = refs[len(refs) - 3 :]
    rows, tokens = place.shape

    @pl.when(pl.program_id(0) == 0)
    def _():
        wide = jnp.broadcast_to(w_ref[...][:, None, :], (PLANE, per_dest, tokens)).reshape(rows, tokens)
        place[...] = jnp.where(placement(q_ref[...], per_dest), wide, 0.0).astype(BF)

    at = 0
    for ref in blocks:
        size = ref.shape[0]
        x_ref[at : at + size, :] = ref[...]
        at += size
    out_ref[...] = jnp.dot(place[...], x_ref[...], preferred_element_type=F32).astype(BF)


def select_cot(q, w, blocks, per_dest, count):
    rows = PLANE * per_dest
    tokens = count * TOK
    small = pl.BlockSpec((PLANE, tokens), lambda i: (0, 0))
    return pl.pallas_call(
        functools.partial(select_cot_body, per_dest, count),
        grid=(D // COLS,),
        in_specs=[small, small]
        + [pl.BlockSpec((b.shape[0], COLS), lambda i: (0, i)) for b in blocks],
        out_specs=pl.BlockSpec((rows, COLS), lambda i: (0, i)),
        out_shape=far_memory((rows, D)),
        scratch_shapes=[pltpu.VMEM((rows, tokens), BF), pltpu.VMEM((tokens, COLS), BF)],
        compiler_params=params(),
        cost_estimate=cost(2 * rows * tokens * D, 2 * D * (rows + tokens)),
        name="select_cotangents",
    )(q, w, *blocks)


def resident():
    return pl.BlockSpec(memory_space=pltpu.VMEM)


def join_body(g_ref, u_ref, d_ref, out_ref, down_ref):
    out_ref[:, 0:FF] = g_ref[...]
    out_ref[:, FF : 2 * FF] = u_ref[...]
    down_ref[...] = d_ref[...]


def join_weights(weights):
    rows = D // 2

    def part(which):
        return pl.BlockSpec((None, None, rows, FF), lambda i: (which, 0, i, 0))

    return pl.pallas_call(
        join_body,
        grid=(2,),
        in_specs=[part(0), part(1), part(2)],
        out_specs=[
            pl.BlockSpec((rows, 2 * FF), lambda i: (i, 0)),
            pl.BlockSpec((rows, FF), lambda i: (i, 0)),
        ],
        out_shape=[jax.ShapeDtypeStruct((D, 2 * FF), BF), jax.ShapeDtypeStruct((D, FF), BF)],
        compiler_params=params(),
        cost_estimate=cost(0, 12 * D * FF),
        name="join_weights",
    )(weights, weights, weights)


def forward_body(x_ref, w_ref, p_ref):
    p_ref[...] = jnp.dot(x_ref[...], w_ref[...], preferred_element_type=F32)


def forward(x, joined, tile):
    rows = x.shape[0]
    return pl.pallas_call(
        forward_body,
        grid=(rows // tile,),
        in_specs=[pl.BlockSpec((tile, D), lambda i: (i, 0)), resident()],
        out_specs=pl.BlockSpec((tile, 2 * FF), lambda i: (i, 0)),
        out_shape=far_memory((rows, 2 * FF), F32),
        compiler_params=params(),
        cost_estimate=cost(4 * rows * D * FF, 2 * D * (rows + 2 * FF)),
        name="expert_forward",
    )(*pinned(x), joined)


def backward_body(per_dest, gate_row, sc_ref, p_ref, w_ref, wd_ref, rows_ref, d_ref, h_ref):
    tile = sc_ref.shape[0]
    back = jnp.dot(sc_ref[...], wd_ref[...], preferred_element_type=F32)
    gate = p_ref[:, 0:FF]
    up = p_ref[:, FF : 2 * FF]
    sig = jax.nn.sigmoid(gate)
    silu = gate * sig
    hidden = (silu * up).astype(BF)
    d_gate = (back * up * sig * (1.0 + gate * (1.0 - sig))).astype(BF)
    d_up = (back * silu).astype(BF)
    h_ref[...] = hidden
    d_ref[:, 0:FF] = d_gate
    d_ref[:, FF : 2 * FF] = d_up
    by_ff = (((1,), (1,)), ((), ()))
    rows_ref[...] = lax.dot_general(d_ref[...], w_ref[...], by_ff, preferred_element_type=F32).astype(BF)
    product = hidden.astype(F32) * back
    high = product.astype(BF)
    low = (product - high.astype(F32)).astype(BF)
    ones = jnp.ones((16, FF), BF)
    line = lax.broadcasted_iota(jnp.int32, (16, per_dest), 0)
    for d in range(tile // per_dest):
        own = slice(d * per_dest, (d + 1) * per_dest)
        part = lax.dot_general(ones, high[own], by_ff, preferred_element_type=F32)
        part += lax.dot_general(ones, low[own], by_ff, preferred_element_type=F32)
        row = d * per_dest + gate_row
        at = row // 16 * 16
        window = rows_ref[at : at + 16, 0:per_dest].astype(F32)
        rows_ref[at : at + 16, 0:per_dest] = jnp.where(line == row - at, part, window).astype(BF)


def backward(scaled, pre, joined, down, tile, per_dest, gate_row):
    rows = scaled.shape[0]
    wide = pl.BlockSpec((tile, D), lambda i: (i, 0))
    slim = pl.BlockSpec((tile, FF), lambda i: (i, 0))
    return pl.pallas_call(
        functools.partial(backward_body, per_dest, gate_row),
        grid=(rows // tile,),
        in_specs=[
            wide,
            pl.BlockSpec((tile, 2 * FF), lambda i: (i, 0)),
            resident(),
            resident(),
        ],
        out_specs=[wide, pl.BlockSpec((tile, 2 * FF), lambda i: (i, 0)), slim],
        out_shape=[
            far_memory((rows, D)),
            far_memory((rows, 2 * FF)),
            far_memory((rows, FF)),
        ],
        compiler_params=params(),
        cost_estimate=cost(6 * rows * D * FF, 4 * D * rows + 6 * D * FF),
        name="expert_backward",
    )(*pinned(scaled, pre), joined, down)


def weight_grad_body(sec_ref, xn, xf, sn, sf, dn, df, hn, hf, sent_ref, kept_ref):
    by_rows = (((0,), (0,)), ((), ()))

    def both(a, b, c, d):
        return (
            lax.dot_general(a[...], c[...], by_rows, preferred_element_type=F32)
            + lax.dot_general(b[...], d[...], by_rows, preferred_element_type=F32)
        ).astype(BF)

    inner = both(xn, xf, dn, df)
    outer = both(sn, sf, hn, hf)

    def store(ref):
        ref[0] = inner[:, 0:FF]
        ref[1] = inner[:, FF : 2 * FF]
        ref[2] = outer

    pl.when(pl.program_id(0) < 2)(lambda: store(sent_ref))
    pl.when(pl.program_id(0) >= 2)(lambda: store(kept_ref))


def weight_grad(section, near, far):
    tile = D // 4
    args, specs = [], []
    for a, b in zip(near, far):
        for v in (a, b):
            args.append(v)
            if v.shape[1] == D:
                specs.append(
                    pl.BlockSpec(
                        (v.shape[0], tile), lambda i, sec: (0, sec[0] ^ (2 * i + 1 - 5 * (i // 2)))
                    )
                )
            else:
                specs.append(pl.BlockSpec(v.shape, lambda i, sec: (0, 0)))
    rows = near[0].shape[0] + far[0].shape[0]
    out = far_memory((2, 3, tile, FF))
    return pl.pallas_call(
        weight_grad_body,
        grid_spec=pltpu.PrefetchScalarGridSpec(
            num_scalar_prefetch=1,
            grid=(4,),
            in_specs=specs,
            out_specs=[
                pl.BlockSpec((None, 3, tile, FF), lambda i, sec: (jnp.minimum(i, 1), 0, 0, 0)),
                pl.BlockSpec((None, 3, tile, FF), lambda i, sec: (jnp.maximum(i - 2, 0), 0, 0, 0)),
            ],
        ),
        out_shape=[out, out],
        compiler_params=params(),
        cost_estimate=cost(6 * rows * D * FF, 4 * rows * D + 6 * D * FF),
        name="weight_grads",
    )(section, *pinned(*args))


def section_mean(sent, kept, back):
    other_core = [(s, s ^ 1) for s in range(4)]
    other_chip = [(s, s ^ 2) for s in range(4)]
    got = lax.ppermute(sent, "section", other_core)
    onward = added(kept[1], got[1])
    onward, back = ordered(onward, back)
    half = onward.shape[1] // 2
    first = lax.ppermute(onward[:, :half], "section", other_chip)
    second = lax.ppermute(onward[:, half:], "section", other_chip)
    return (kept[0], got[0], first, second), back


def mean_of(own, core, first, second):
    chip = jnp.concatenate([first, second], axis=1)
    total = own.astype(F32) + core.astype(F32) + chip.astype(F32)
    return (total / 4.0)[:, None]


def combine_body(per_dest, count, gate_row, z_ref, q_ref, w_ref, r_ref, x_ref, *refs):
    place = refs[-1]
    outs = refs[:-1]
    rows, tokens = place.shape
    first_step = pl.program_id(0) == 0

    @pl.when(first_step)
    def _():
        place[...] = jnp.where(placement(q_ref[...], per_dest), 1.0, 0.0).astype(BF)

    summed = lax.dot_general(
        place[...], x_ref[...], (((0,), (0,)), ((), ())), preferred_element_type=F32
    ).astype(BF)
    at = 0
    for ref in outs:
        size = ref.shape[0] if ref.shape[0] == HALF else ref.shape[0] - META
        ref[0:size, :] = summed[at : at + size, :]
        if ref.shape[0] != HALF:
            ref[size : size + META, :] = jnp.zeros((META, COLS), BF)
        at += size

    @pl.when(first_step)
    def _():
        first = z_ref[0] // PLANE * PLANE
        find = (
            lax.broadcasted_iota(jnp.int32, (PLANE, rows), 1)
            == lax.broadcasted_iota(jnp.int32, (PLANE, rows), 0) * per_dest + gate_row
        )
        gates = jnp.dot(
            jnp.where(find, 1.0, 0.0).astype(BF), x_ref[:, 0:TOK], preferred_element_type=F32
        )
        by_code = jnp.zeros((PLANE, tokens), F32)
        line = lax.broadcasted_iota(jnp.int32, (PLANE, TOK), 0)
        lane = lax.broadcasted_iota(jnp.int32, (PLANE, TOK), 1)
        code = lax.broadcasted_iota(jnp.int32, (TOK, tokens), 0)
        for j in range(PLANE):
            own = jnp.where((line == j) & (lane < count * CAP), gates, 0.0).astype(BF)
            hit = jnp.where(code == q_ref[j : j + 1, :], 1.0, 0.0).astype(BF)
            by_code = by_code + jnp.dot(own, hit, preferred_element_type=F32)
        weight = w_ref[...]
        by_code = jnp.where(weight > 0.0, by_code / jnp.where(weight > 0.0, weight, 1.0), 0.0)
        routes = r_ref[...]
        by_k = jnp.zeros((PLANE, tokens), F32)
        for j in range(PLANE):
            mine = routes == (first + j).astype(F32)
            by_k = jnp.where(mine, by_code[j : j + 1, :], by_k)
        b = 0
        for ref in outs:
            if ref.shape[0] == HALF:
                continue
            size = ref.shape[0] - META
            ref[size : size + META, 0:TOK] = by_k[:, b * TOK : (b + 1) * TOK].astype(BF)
            b += 1


def combine(z, q, w, r, x, sizes, per_dest, count, gate_row):
    rows = PLANE * per_dest
    tokens = count * TOK
    small = pl.BlockSpec((PLANE, tokens), lambda i: (0, 0))
    return pl.pallas_call(
        functools.partial(combine_body, per_dest, count, gate_row),
        grid=(D // COLS,),
        in_specs=[
            pl.BlockSpec(memory_space=pltpu.SMEM),
            small,
            small,
            small,
            pl.BlockSpec((rows, COLS), lambda i: (0, i)),
        ],
        out_specs=[pl.BlockSpec((n, COLS), lambda i: (0, i)) for n in sizes],
        out_shape=[far_memory((n, D)) for n in sizes],
        scratch_shapes=[pltpu.VMEM((rows, tokens), BF)],
        compiler_params=params(),
        cost_estimate=cost(2 * rows * tokens * D, 2 * D * (rows + tokens)),
        name="combine_rows",
    )(z, q, w, r, x)


def ring_gather(own):
    fw, bw = forward_pairs(), backward_pairs()
    got = {0: own}
    down = up = own
    for step in (1, 2, 3):
        down = lax.ppermute(down, "expert", fw)
        up = lax.ppermute(up, "expert", bw)
        got[-step], got[step] = down, up
    top = lax.ppermute(down[:HALF], "expert", fw)
    low = lax.ppermute(up[HALF:], "expert", bw)
    near = [got[k] for k in NEAR]
    far = [got[k] for k in FAR[:-1]] + [top, low]
    return near, far


def added(a, b):
    return (a.astype(F32) + b.astype(F32)).astype(BF)


def ring_scatter(near, far):
    fw, bw = forward_pairs(), backward_pairs()
    part = dict(zip(NEAR, near)) | dict(zip(FAR[:-1], far[:-2]))
    top = lax.ppermute(far[-2], "expert", fw)
    low = lax.ppermute(far[-1], "expert", bw)
    ahead = added(part[3], jnp.pad(top, ((0, META + HALF), (0, 0))))
    behind = added(part[-3], jnp.pad(low, ((HALF, 0), (0, 0))))
    for step in (2, 1):
        ahead = added(part[step], lax.ppermute(ahead, "expert", fw))
        behind = added(part[-step], lax.ppermute(behind, "expert", bw))
    ahead = lax.ppermute(ahead, "expert", fw)
    behind = lax.ppermute(behind, "expert", bw)
    return part[0].astype(F32) + ahead.astype(F32) + behind.astype(F32)


def per_device(tokens, cotangent, routes, route_weights, weights):
    z = lax.axis_index("expert").reshape(1).astype(jnp.int32)
    section = lax.axis_index("section").reshape(1).astype(jnp.int32)
    own = pack(tokens[0], routes[0].T, route_weights[0].T)
    tok_near, tok_far = ring_gather(own)
    joined, down = join_weights(weights)
    cot, tok_near[1], tok_near[2] = ordered(cotangent[0], tok_near[1], tok_near[2])
    cot_near, cot_far = ring_gather(cot)

    send, qn, wn, rn = select_tok(z, tok_near, NEAR_ROWS, len(NEAR))
    xn = exchange(send, NEAR_ROWS)
    send = select_cot(qn, wn, cot_near, NEAR_ROWS, len(NEAR))
    send, xn, tok_far[0], tok_far[1] = ordered(send, xn, tok_far[0], tok_far[1])
    sn = exchange(send, NEAR_ROWS)
    send, qf, wf, rf = select_tok(z, tok_far, FAR_ROWS, len(FAR))
    send, sn = ordered(send, sn)
    xf = exchange(send, FAR_ROWS)
    send, xf = ordered(select_cot(qf, wf, cot_far, FAR_ROWS, len(FAR)), xf)
    sf = exchange(send, FAR_ROWS)

    near_tile, far_tile = 4 * NEAR_ROWS, 4 * FAR_ROWS
    pn = forward(xn, joined, near_tile)
    pf = forward(xf, joined, far_tile)
    near_gate, far_gate = len(NEAR) * CAP, len(FAR) * CAP
    rows_n, dn, hn = backward(sn, pn, joined, down, near_tile, NEAR_ROWS, near_gate)
    sf, rows_n, pf = ordered(sf, rows_n, pf)
    rows_f, df, hf = backward(sf, pf, joined, down, far_tile, FAR_ROWS, far_gate)
    back_f = exchange(rows_f, FAR_ROWS)
    rows_n, back_f = ordered(rows_n, back_f)
    back_n = exchange(rows_n, NEAR_ROWS)

    sent, kept = weight_grad(section, (xn, sn, dn, hn), (xf, sf, df, hf))
    (mine, core, first, second), back_f = section_mean(sent, kept, back_f)
    far_sizes = [ROWS] * 4 + [HALF, HALF + META]
    far_parts = list(combine(z, qf, wf, rf, back_f, far_sizes, FAR_ROWS, len(FAR), far_gate))
    far_parts[3], first = ordered(far_parts[3], first)
    far_parts[1], second = ordered(far_parts[1], second)
    near_parts = combine(z, qn, wn, rn, back_n, [ROWS] * 3, NEAR_ROWS, len(NEAR), near_gate)
    total = ring_scatter(near_parts, far_parts)
    token_grads = total[:TOK].astype(BF)[None]
    gate_grads = total[TOK:, :TOK].T.astype(BF)[None]
    return token_grads, gate_grads, mean_of(mine, core, first, second)


def solution(mesh):
    placed = (
        P("section", "expert", None),
        P("section", "expert", None),
        P("section", "expert", None),
        P("section", "expert", None),
        P(None, "expert", None, None),
    )
    return jax.shard_map(
        per_device,
        mesh=mesh,
        in_specs=placed,
        out_specs=(
            P("section", "expert", None),
            P("section", "expert", None),
            P(None, "expert", "section", None),
        ),
        check_vma=False,
    )
```

```python
import functools

import jax
import jax.numpy as jnp
from jax import lax
from jax.experimental import pallas as pl
from jax.experimental.pallas import tpu as pltpu
from jax.sharding import PartitionSpec as P

D = 2048
FF = 384
TOP_K = 8
TOK = 128
CAP = 18
PLANES = 8
PLANE = 8
META = 8
ROWS = TOK + META
HALF = 64
NEAR = (0, -1, 1)
FAR = (-2, 2, -3, 3, 4)
NEAR_ROWS = 56
FAR_ROWS = 96
COLS = 1024
BF = jnp.bfloat16
F32 = jnp.float32
VMEM_LIMIT = 32 * 1024 * 1024


def params():
    return pltpu.CompilerParams(vmem_limit_bytes=VMEM_LIMIT)


def cost(flops, nbytes):
    return pl.CostEstimate(flops=flops, bytes_accessed=nbytes, transcendentals=0)


def far_memory(shape, dtype=BF):
    return pltpu.HBM(shape, dtype)


def pinned(*arrays):
    return [pltpu.with_memory_space_constraint(a, pltpu.HBM) for a in arrays]


def forward_pairs():
    return [(e, (e + PLANE) % (PLANES * PLANE)) for e in range(PLANES * PLANE)]


def backward_pairs():
    return [(e, (e - PLANE) % (PLANES * PLANE)) for e in range(PLANES * PLANE)]


def ordered(*values):
    return lax.optimization_barrier(values)


def plane_groups():
    groups = []
    for parity in range(2):
        for core in range(2):
            for z in range(PLANES):
                groups.append(
                    [
                        ((parity ^ (j % 2)) * 2 + core) * 64 + z * PLANE + j
                        for j in range(PLANE)
                    ]
                )
    return groups


def exchange(rows, per_dest):
    sent = rows.reshape(PLANE, per_dest, D)
    got = lax.all_to_all(
        sent, ("section", "expert"), 0, 0, axis_index_groups=plane_groups(), tiled=True
    )
    return got.reshape(PLANE * per_dest, D)


def pack_body(tok_ref, routes_ref, weight_ref, out_ref):
    out_ref[0:TOK, :] = tok_ref[...]
    out_ref[TOK:ROWS, :] = jnp.concatenate(
        [routes_ref[...].astype(F32), weight_ref[...].astype(F32), jnp.zeros((META, D - 2 * TOK), F32)],
        axis=1,
    ).astype(BF)


def pack(tok, routes_t, weight_t):
    return pl.pallas_call(
        pack_body,
        out_shape=jax.ShapeDtypeStruct((ROWS, D), BF),
        compiler_params=params(),
        cost_estimate=cost(0, 4 * ROWS * D),
        name="pack_rows",
    )(tok, routes_t, weight_t)


def placement(q, per_dest):
    tokens = q.shape[1]
    rows = PLANE * per_dest
    wide = jnp.broadcast_to(q[:, None, :], (PLANE, per_dest, tokens)).reshape(rows, tokens)
    code = lax.broadcasted_iota(jnp.int32, (PLANE, per_dest, tokens), 1).reshape(rows, tokens)
    return wide == code


def select_tok_body(per_dest, count, z_ref, *refs):
    blocks = refs[: len(refs) - 6]
    out_ref, q_ref, w_ref, r_ref, place, x_ref = refs[len(refs) - 6 :]
    split = count == len(FAR)
    metas = [b for b in blocks if b.shape[0] != HALF]

    @pl.when(pl.program_id(0) == 0)
    def _():
        first = z_ref[0] // PLANE * PLANE
        ids = lax.broadcasted_iota(jnp.int32, (PLANE, TOK), 0) + first
        earlier = (
            lax.broadcasted_iota(jnp.int32, (TOK, TOK), 0)
            < lax.broadcasted_iota(jnp.int32, (TOK, TOK), 1)
        ).astype(F32).astype(BF)
        for b, ref in enumerate(metas):
            base = ref.shape[0] - META
            routes = ref[base : base + META, 0:TOK].astype(F32)
            weight = ref[base : base + META, TOK : 2 * TOK].astype(F32)
            ids_f = ids.astype(F32)
            member = jnp.zeros((PLANE, TOK), F32)
            scale = jnp.zeros((PLANE, TOK), F32)
            for k in range(TOP_K):
                hit = ids_f == routes[k : k + 1, :]
                member = jnp.where(hit, 1.0, member)
                scale = jnp.where(hit, weight[k : k + 1, :], scale)
            slot = jnp.dot(member.astype(BF), earlier, preferred_element_type=F32)
            q = jnp.where(member > 0.0, slot + float(b * CAP), -1.0).astype(jnp.int32)
            q_ref[:, b * TOK : (b + 1) * TOK] = q
            w_ref[:, b * TOK : (b + 1) * TOK] = scale
            r_ref[:, b * TOK : (b + 1) * TOK] = routes
        place[...] = jnp.where(placement(q_ref[...], per_dest), 1.0, 0.0).astype(BF)

    at = 0
    for ref in blocks:
        size = HALF if split and ref.shape[0] in (HALF, HALF + META) else TOK
        x_ref[at : at + size, :] = ref[0:size, :]
        at += size
    out_ref[...] = jnp.dot(place[...], x_ref[...], preferred_element_type=F32).astype(BF)


def select_tok(z, blocks, per_dest, count):
    rows = PLANE * per_dest
    tokens = count * TOK
    const = lambda i: (0, 0)
    small = pl.BlockSpec((PLANE, tokens), const)
    return pl.pallas_call(
        functools.partial(select_tok_body, per_dest, count),
        grid=(D // COLS,),
        in_specs=[pl.BlockSpec(memory_space=pltpu.SMEM)]
        + [pl.BlockSpec((b.shape[0], COLS), lambda i: (0, i)) for b in blocks],
        out_specs=[pl.BlockSpec((rows, COLS), lambda i: (0, i)), small, small, small],
        out_shape=[
            far_memory((rows, D)),
            jax.ShapeDtypeStruct((PLANE, tokens), jnp.int32),
            jax.ShapeDtypeStruct((PLANE, tokens), F32),
            jax.ShapeDtypeStruct((PLANE, tokens), F32),
        ],
        scratch_shapes=[pltpu.VMEM((rows, tokens), BF), pltpu.VMEM((tokens, COLS), BF)],
        compiler_params=params(),
        cost_estimate=cost(2 * rows * tokens * D, 2 * D * (rows + tokens)),
        name="select_tokens",
    )(z, *blocks)


def select_cot_body(per_dest, count, q_ref, w_ref, *refs):
    blocks = refs[: len(refs) - 3]
    out_ref, place, x_ref = refs[len(refs) - 3 :]
    rows, tokens = place.shape

    @pl.when(pl.program_id(0) == 0)
    def _():
        wide = jnp.broadcast_to(w_ref[...][:, None, :], (PLANE, per_dest, tokens)).reshape(rows, tokens)
        place[...] = jnp.where(placement(q_ref[...], per_dest), wide, 0.0).astype(BF)

    at = 0
    for ref in blocks:
        size = ref.shape[0]
        x_ref[at : at + size, :] = ref[...]
        at += size
    out_ref[...] = jnp.dot(place[...], x_ref[...], preferred_element_type=F32).astype(BF)


def select_cot(q, w, blocks, per_dest, count):
    rows = PLANE * per_dest
    tokens = count * TOK
    small = pl.BlockSpec((PLANE, tokens), lambda i: (0, 0))
    return pl.pallas_call(
        functools.partial(select_cot_body, per_dest, count),
        grid=(D // COLS,),
        in_specs=[small, small]
        + [pl.BlockSpec((b.shape[0], COLS), lambda i: (0, i)) for b in blocks],
        out_specs=pl.BlockSpec((rows, COLS), lambda i: (0, i)),
        out_shape=far_memory((rows, D)),
        scratch_shapes=[pltpu.VMEM((rows, tokens), BF), pltpu.VMEM((tokens, COLS), BF)],
        compiler_params=params(),
        cost_estimate=cost(2 * rows * tokens * D, 2 * D * (rows + tokens)),
        name="select_cotangents",
    )(q, w, *blocks)


def resident():
    return pl.BlockSpec(memory_space=pltpu.VMEM)


def join_body(g_ref, u_ref, d_ref, out_ref, down_ref):
    out_ref[:, 0:FF] = g_ref[...]
    out_ref[:, FF : 2 * FF] = u_ref[...]
    down_ref[...] = d_ref[...]


def join_weights(weights):
    rows = D // 2

    def part(which):
        return pl.BlockSpec((None, None, rows, FF), lambda i: (which, 0, i, 0))

    return pl.pallas_call(
        join_body,
        grid=(2,),
        in_specs=[part(0), part(1), part(2)],
        out_specs=[
            pl.BlockSpec((rows, 2 * FF), lambda i: (i, 0)),
            pl.BlockSpec((rows, FF), lambda i: (i, 0)),
        ],
        out_shape=[jax.ShapeDtypeStruct((D, 2 * FF), BF), jax.ShapeDtypeStruct((D, FF), BF)],
        compiler_params=params(),
        cost_estimate=cost(0, 12 * D * FF),
        name="join_weights",
    )(weights, weights, weights)


def forward_body(x_ref, w_ref, p_ref):
    p_ref[...] = jnp.dot(x_ref[...], w_ref[...], preferred_element_type=F32)


def forward(x, joined, tile):
    rows = x.shape[0]
    return pl.pallas_call(
        forward_body,
        grid=(rows // tile,),
        in_specs=[pl.BlockSpec((tile, D), lambda i: (i, 0)), resident()],
        out_specs=pl.BlockSpec((tile, 2 * FF), lambda i: (i, 0)),
        out_shape=far_memory((rows, 2 * FF), F32),
        compiler_params=params(),
        cost_estimate=cost(4 * rows * D * FF, 2 * D * (rows + 2 * FF)),
        name="expert_forward",
    )(*pinned(x), joined)


def backward_body(per_dest, gate_row, sc_ref, p_ref, w_ref, wd_ref, rows_ref, d_ref, h_ref):
    tile = sc_ref.shape[0]
    back = jnp.dot(sc_ref[...], wd_ref[...], preferred_element_type=F32)
    gate = p_ref[:, 0:FF]
    up = p_ref[:, FF : 2 * FF]
    sig = jax.nn.sigmoid(gate)
    silu = gate * sig
    hidden = (silu * up).astype(BF)
    d_gate = (back * up * sig * (1.0 + gate * (1.0 - sig))).astype(BF)
    d_up = (back * silu).astype(BF)
    h_ref[...] = hidden
    d_ref[:, 0:FF] = d_gate
    d_ref[:, FF : 2 * FF] = d_up
    by_ff = (((1,), (1,)), ((), ()))
    rows_ref[...] = lax.dot_general(d_ref[...], w_ref[...], by_ff, preferred_element_type=F32).astype(BF)
    product = hidden.astype(F32) * back
    high = product.astype(BF)
    low = (product - high.astype(F32)).astype(BF)
    ones = jnp.ones((16, FF), BF)
    line = lax.broadcasted_iota(jnp.int32, (16, per_dest), 0)
    for d in range(tile // per_dest):
        own = slice(d * per_dest, (d + 1) * per_dest)
        part = lax.dot_general(ones, high[own], by_ff, preferred_element_type=F32)
        part += lax.dot_general(ones, low[own], by_ff, preferred_element_type=F32)
        row = d * per_dest + gate_row
        at = row // 16 * 16
        window = rows_ref[at : at + 16, 0:per_dest].astype(F32)
        rows_ref[at : at + 16, 0:per_dest] = jnp.where(line == row - at, part, window).astype(BF)


def backward(scaled, pre, joined, down, tile, per_dest, gate_row):
    rows = scaled.shape[0]
    wide = pl.BlockSpec((tile, D), lambda i: (i, 0))
    slim = pl.BlockSpec((tile, FF), lambda i: (i, 0))
    return pl.pallas_call(
        functools.partial(backward_body, per_dest, gate_row),
        grid=(rows // tile,),
        in_specs=[
            wide,
            pl.BlockSpec((tile, 2 * FF), lambda i: (i, 0)),
            resident(),
            resident(),
        ],
        out_specs=[wide, pl.BlockSpec((tile, 2 * FF), lambda i: (i, 0)), slim],
        out_shape=[
            far_memory((rows, D)),
            far_memory((rows, 2 * FF)),
            far_memory((rows, FF)),
        ],
        compiler_params=params(),
        cost_estimate=cost(6 * rows * D * FF, 4 * D * rows + 6 * D * FF),
        name="expert_backward",
    )(*pinned(scaled, pre), joined, down)


def weight_grad_body(sec_ref, xn, xf, sn, sf, dn, df, hn, hf, sent_ref, kept_ref):
    by_rows = (((0,), (0,)), ((), ()))

    def both(a, b, c, d):
        return (
            lax.dot_general(a[...], c[...], by_rows, preferred_element_type=F32)
            + lax.dot_general(b[...], d[...], by_rows, preferred_element_type=F32)
        ).astype(BF)

    inner = both(xn, xf, dn, df)
    outer = both(sn, sf, hn, hf)

    def store(ref):
        ref[0] = inner[:, 0:FF]
        ref[1] = inner[:, FF : 2 * FF]
        ref[2] = outer

    pl.when(pl.program_id(0) < 2)(lambda: store(sent_ref))
    pl.when(pl.program_id(0) >= 2)(lambda: store(kept_ref))


def weight_grad(section, near, far):
    tile = D // 4
    args, specs = [], []
    for a, b in zip(near, far):
        for v in (a, b):
            args.append(v)
            if v.shape[1] == D:
                specs.append(
                    pl.BlockSpec(
                        (v.shape[0], tile), lambda i, sec: (0, sec[0] ^ (2 * i + 1 - 5 * (i // 2)))
                    )
                )
            else:
                specs.append(pl.BlockSpec(v.shape, lambda i, sec: (0, 0)))
    rows = near[0].shape[0] + far[0].shape[0]
    out = far_memory((2, 3, tile, FF))
    return pl.pallas_call(
        weight_grad_body,
        grid_spec=pltpu.PrefetchScalarGridSpec(
            num_scalar_prefetch=1,
            grid=(4,),
            in_specs=specs,
            out_specs=[
                pl.BlockSpec((None, 3, tile, FF), lambda i, sec: (jnp.minimum(i, 1), 0, 0, 0)),
                pl.BlockSpec((None, 3, tile, FF), lambda i, sec: (jnp.maximum(i - 2, 0), 0, 0, 0)),
            ],
        ),
        out_shape=[out, out],
        compiler_params=params(),
        cost_estimate=cost(6 * rows * D * FF, 4 * rows * D + 6 * D * FF),
        name="weight_grads",
    )(section, *pinned(*args))


def section_mean(sent, kept, back):
    other_core = [(s, s ^ 1) for s in range(4)]
    other_chip = [(s, s ^ 2) for s in range(4)]
    got = lax.ppermute(sent, "section", other_core)
    onward = added(kept[1], got[1])
    onward, back = ordered(onward, back)
    half = onward.shape[1] // 2
    first = lax.ppermute(onward[:, :half], "section", other_chip)
    second = lax.ppermute(onward[:, half:], "section", other_chip)
    return (kept[0], got[0], first, second), back


def mean_of(own, core, first, second):
    chip = jnp.concatenate([first, second], axis=1)
    total = own.astype(F32) + core.astype(F32) + chip.astype(F32)
    return (total / 4.0)[:, None]


def combine_body(per_dest, count, gate_row, z_ref, q_ref, w_ref, r_ref, x_ref, *refs):
    place = refs[-1]
    outs = refs[:-1]
    rows, tokens = place.shape
    first_step = pl.program_id(0) == 0

    @pl.when(first_step)
    def _():
        place[...] = jnp.where(placement(q_ref[...], per_dest), 1.0, 0.0).astype(BF)

    summed = lax.dot_general(
        place[...], x_ref[...], (((0,), (0,)), ((), ())), preferred_element_type=F32
    ).astype(BF)
    at = 0
    for ref in outs:
        size = ref.shape[0] if ref.shape[0] == HALF else ref.shape[0] - META
        ref[0:size, :] = summed[at : at + size, :]
        if ref.shape[0] != HALF:
            ref[size : size + META, :] = jnp.zeros((META, COLS), BF)
        at += size

    @pl.when(first_step)
    def _():
        first = z_ref[0] // PLANE * PLANE
        find = (
            lax.broadcasted_iota(jnp.int32, (PLANE, rows), 1)
            == lax.broadcasted_iota(jnp.int32, (PLANE, rows), 0) * per_dest + gate_row
        )
        gates = jnp.dot(
            jnp.where(find, 1.0, 0.0).astype(BF), x_ref[:, 0:TOK], preferred_element_type=F32
        )
        by_code = jnp.zeros((PLANE, tokens), F32)
        line = lax.broadcasted_iota(jnp.int32, (PLANE, TOK), 0)
        lane = lax.broadcasted_iota(jnp.int32, (PLANE, TOK), 1)
        code = lax.broadcasted_iota(jnp.int32, (TOK, tokens), 0)
        for j in range(PLANE):
            own = jnp.where((line == j) & (lane < count * CAP), gates, 0.0).astype(BF)
            hit = jnp.where(code == q_ref[j : j + 1, :], 1.0, 0.0).astype(BF)
            by_code = by_code + jnp.dot(own, hit, preferred_element_type=F32)
        weight = w_ref[...]
        by_code = jnp.where(weight > 0.0, by_code / jnp.where(weight > 0.0, weight, 1.0), 0.0)
        routes = r_ref[...]
        by_k = jnp.zeros((PLANE, tokens), F32)
        for j in range(PLANE):
            mine = routes == (first + j).astype(F32)
            by_k = jnp.where(mine, by_code[j : j + 1, :], by_k)
        b = 0
        for ref in outs:
            if ref.shape[0] == HALF:
                continue
            size = ref.shape[0] - META
            ref[size : size + META, 0:TOK] = by_k[:, b * TOK : (b + 1) * TOK].astype(BF)
            b += 1


def combine(z, q, w, r, x, sizes, per_dest, count, gate_row):
    rows = PLANE * per_dest
    tokens = count * TOK
    small = pl.BlockSpec((PLANE, tokens), lambda i: (0, 0))
    return pl.pallas_call(
        functools.partial(combine_body, per_dest, count, gate_row),
        grid=(D // COLS,),
        in_specs=[
            pl.BlockSpec(memory_space=pltpu.SMEM),
            small,
            small,
            small,
            pl.BlockSpec((rows, COLS), lambda i: (0, i)),
        ],
        out_specs=[pl.BlockSpec((n, COLS), lambda i: (0, i)) for n in sizes],
        out_shape=[far_memory((n, D)) for n in sizes],
        scratch_shapes=[pltpu.VMEM((rows, tokens), BF)],
        compiler_params=params(),
        cost_estimate=cost(2 * rows * tokens * D, 2 * D * (rows + tokens)),
        name="combine_rows",
    )(z, q, w, r, x)


def ring_gather(own):
    fw, bw = forward_pairs(), backward_pairs()
    got = {0: own}
    down = up = own
    for step in (1, 2, 3):
        down = lax.ppermute(down, "expert", fw)
        up = lax.ppermute(up, "expert", bw)
        got[-step], got[step] = down, up
    top = lax.ppermute(down[:HALF], "expert", fw)
    low = lax.ppermute(up[HALF:], "expert", bw)
    near = [got[k] for k in NEAR]
    far = [got[k] for k in FAR[:-1]] + [top, low]
    return near, far


def added(a, b):
    return (a.astype(F32) + b.astype(F32)).astype(BF)


def ring_scatter(near, far):
    fw, bw = forward_pairs(), backward_pairs()
    part = dict(zip(NEAR, near)) | dict(zip(FAR, far))
    ahead, behind = part[4], part[-3]
    for step in (3, 2, 1):
        ahead = added(part[step], lax.ppermute(ahead, "expert", fw))
        if step < 3:
            behind = added(part[-step], lax.ppermute(behind, "expert", bw))
    ahead = lax.ppermute(ahead, "expert", fw)
    behind = lax.ppermute(behind, "expert", bw)
    return part[0].astype(F32) + ahead.astype(F32) + behind.astype(F32)


def per_device(tokens, cotangent, routes, route_weights, weights):
    z = lax.axis_index("expert").reshape(1).astype(jnp.int32)
    section = lax.axis_index("section").reshape(1).astype(jnp.int32)
    own = pack(tokens[0], routes[0].T, route_weights[0].T)
    tok_near, tok_far = ring_gather(own)
    joined, down = join_weights(weights)
    cot, tok_near[1], tok_near[2] = ordered(cotangent[0], tok_near[1], tok_near[2])
    cot_near, cot_far = ring_gather(cot)

    send, qn, wn, rn = select_tok(z, tok_near, NEAR_ROWS, len(NEAR))
    xn = exchange(send, NEAR_ROWS)
    send = select_cot(qn, wn, cot_near, NEAR_ROWS, len(NEAR))
    send, xn, tok_far[0], tok_far[1] = ordered(send, xn, tok_far[0], tok_far[1])
    sn = exchange(send, NEAR_ROWS)
    send, qf, wf, rf = select_tok(z, tok_far, FAR_ROWS, len(FAR))
    send, sn = ordered(send, sn)
    xf = exchange(send, FAR_ROWS)
    send, xf = ordered(select_cot(qf, wf, cot_far, FAR_ROWS, len(FAR)), xf)
    sf = exchange(send, FAR_ROWS)

    near_tile, far_tile = 4 * NEAR_ROWS, 4 * FAR_ROWS
    pn = forward(xn, joined, near_tile)
    pf = forward(xf, joined, far_tile)
    near_gate, far_gate = len(NEAR) * CAP, len(FAR) * CAP
    rows_n, dn, hn = backward(sn, pn, joined, down, near_tile, NEAR_ROWS, near_gate)
    sf, rows_n, pf = ordered(sf, rows_n, pf)
    rows_f, df, hf = backward(sf, pf, joined, down, far_tile, FAR_ROWS, far_gate)
    back_f = exchange(rows_f, FAR_ROWS)
    rows_n, back_f = ordered(rows_n, back_f)
    back_n = exchange(rows_n, NEAR_ROWS)

    sent, kept = weight_grad(section, (xn, sn, dn, hn), (xf, sf, df, hf))
    (mine, core, first, second), back_f = section_mean(sent, kept, back_f)
    far_sizes = [ROWS] * 5
    far_parts = list(combine(z, qf, wf, rf, back_f, far_sizes, FAR_ROWS, len(FAR), far_gate))
    far_parts[3], first = ordered(far_parts[3], first)
    far_parts[1], second = ordered(far_parts[1], second)
    near_parts = combine(z, qn, wn, rn, back_n, [ROWS] * 3, NEAR_ROWS, len(NEAR), near_gate)
    total = ring_scatter(near_parts, far_parts)
    token_grads = total[:TOK].astype(BF)[None]
    gate_grads = total[TOK:, :TOK].T.astype(BF)[None]
    return token_grads, gate_grads, mean_of(mine, core, first, second)


def solution(mesh):
    placed = (
        P("section", "expert", None),
        P("section", "expert", None),
        P("section", "expert", None),
        P("section", "expert", None),
        P(None, "expert", None, None),
    )
    return jax.shard_map(
        per_device,
        mesh=mesh,
        in_specs=placed,
        out_specs=(
            P("section", "expert", None),
            P("section", "expert", None),
            P(None, "expert", "section", None),
        ),
        check_vma=False,
    )
```
